256 devices in a mesh: pipe: 8 (over z), seq: 16 (over x, y), tp: 2 (over core).
Axes of the slice: x: 4, y: 4, z: 8, core: 2. Of those that a mesh axis runs over, the one named last changes fastest.
Arguments:
- layer_inputs: bfloat16 [8, 2048, 4096], P('pipe', ('seq', 'tp')), may hold values from -6 to 6
- out_grad: bfloat16 [2048, 4096], P('seq', 'tp'), may hold values from -6 to 6
- short_weights: bfloat16 [8, 7, 3, 4096], P('pipe', None, None, 'tp'), may hold values from -2 to 2
- long_filters: bfloat16 [8, 256, 128], P('pipe', 'tp'), may hold values from -0.15625 to 0.15625
- out_weights: bfloat16 [8, 4096, 4096], P('pipe', 'tp', 'seq'), may hold values from -0.09375 to 0.09375
Outputs:
- input_grad: bfloat16 [8, 2048, 4096], P('pipe', 'seq', 'tp')
- short_grad: float32 [8, 7, 3, 4096], P('pipe', None, None, 'tp')
- long_grad: float32 [8, 256, 128], P('pipe', 'tp')
The draws below stay inside these ranges and needn't reach their ends.
All inputs are finite; a program needn't handle non-finite values.
Results may differ from the reference program's by a relative error of at most 0.03.
Values may be sent and summed in bfloat16 or wider, within the bound.
No kernel may reach another device: no remote copies, remote signals or barrier semaphores. Data moves between devices by JAX's collectives and lax.ppermute only.
A program may use at most 192 MiB of HBM per device.

```python
import jax
import jax.numpy as jnp
from jax import lax

D = 4096
KL = 128
KS = 7
SECTIONS = 8
TOKENS = 2048
GROUPS = 256


def levels(key, shape, pieces, least, top_value):
    loudness = 1.0
    for dim, parts in pieces:
        heights = jax.random.uniform(jax.random.fold_in(jax.random.fold_in(key, 6), dim), (parts,), jnp.float32, least / len(pieces), top_value / len(pieces))
        loudness = loudness * jnp.repeat(jnp.exp(heights), shape[dim] // parts).reshape((-1,) + (1,) * (len(shape) - 1 - dim))
    return loudness


def scatter_about(stream_key, shape, scale, limit, cuts=(), kind=jnp.bfloat16):
    drawn = scale * jax.random.normal(stream_key, shape, jnp.float32)
    if cuts:
        drawn = drawn * levels(stream_key, shape, cuts, -0.22, 0.18)
    return jnp.clip(drawn, -limit, limit).astype(kind)


def setup_inputs(seed: int = 0) -> dict:
    splits = jax.random.split(jax.random.key(seed), 6)
    return {
        "layer_inputs": scatter_about(splits[0], (SECTIONS, TOKENS, D), 1.0, 6.0, ((0, 8), (1, 32))),
        "out_grad": scatter_about(splits[1], (TOKENS, D), 1.0, 6.0, ((0, 16), (1, 2))),
        "short_weights": scatter_about(splits[2], (SECTIONS, KS, 3, D), KS ** -0.5, 2.0, ((0, 8), (3, 2))),
        "long_filters": scatter_about(splits[3], (SECTIONS, GROUPS, KL), (11 * KL) ** -0.5, 0.15625, ((0, 8), (1, 2))),
        "out_weights": scatter_about(splits[4], (SECTIONS, D, D), D ** -0.5, 0.09375, ((0, 8), (1, 2), (2, 16))),
    }


exact_mode = lax.Precision.HIGHEST


def toeplitz_blocks(filters):
    groups, kernel_width = filters.shape
    base_row = jnp.concatenate([jnp.zeros((groups, 1), filters.dtype), filters[:, ::-1], jnp.zeros((groups, kernel_width), filters.dtype)], axis=1)
    tiled = jnp.tile(base_row, (1, kernel_width))[:, : 2 * kernel_width * kernel_width]
    return tiled.reshape(groups, kernel_width, 2 * kernel_width)


def lag_sums(products):
    groups, kernel_width, window = products.shape
    flattened = products.reshape(groups, kernel_width * window)
    flattened = jnp.pad(flattened, ((0, 0), (0, kernel_width)))
    skewed = flattened.reshape(groups, kernel_width, window + 1)
    totals = jnp.sum(skewed, axis=1)
    return totals[:, 1: kernel_width + 1][:, ::-1]


def featurize(source, weights):
    tap_count = weights.shape[0]
    row_count = source.shape[0] - tap_count + 1
    running = jnp.zeros((weights.shape[1], row_count, source.shape[1]), jnp.float32)
    for offset in range(tap_count):
        start = tap_count - 1 - offset
        running = running + weights[offset][:, None, :] * source[start: start + row_count][None]
    return running


def spread_back(feature_grads, weights):
    tap_count = weights.shape[0]
    row_count = feature_grads.shape[1] - tap_count + 1
    running = jnp.zeros((row_count, feature_grads.shape[2]), jnp.float32)
    for offset in range(tap_count):
        running = running + jnp.sum(weights[offset][:, None, :] * feature_grads[:, offset: offset + row_count], axis=0)
    return running


def weight_grads(feature_grads, source):
    row_count = feature_grads.shape[1]
    tap_count = source.shape[0] - row_count + 1
    terms = []
    for offset in range(tap_count):
        start = tap_count - 1 - offset
        terms.append(jnp.sum(feature_grads * source[start: start + row_count][None], axis=1))
    return jnp.stack(terms)


def long_forward(padded, toeplitz, groups):
    kernel_width = toeplitz.shape[1]
    blocks = padded.astype(jnp.float32).reshape(padded.shape[0] // kernel_width, kernel_width, groups, -1)
    matrix = toeplitz.astype(jnp.float32)
    earlier = jnp.einsum("gij,bjgc->bigc", matrix[:, :, :kernel_width], blocks[:-1], precision=exact_mode)
    current = jnp.einsum("gij,bjgc->bigc", matrix[:, :, kernel_width:], blocks[1:], precision=exact_mode)
    return (earlier + current).reshape(-1, padded.shape[1])


def long_backward(padded, toeplitz, groups):
    kernel_width = toeplitz.shape[1]
    blocks = padded.astype(jnp.float32).reshape(padded.shape[0] // kernel_width, kernel_width, groups, -1)
    matrix = toeplitz.astype(jnp.float32)
    current = jnp.einsum("gij,bigc->bjgc", matrix[:, :, kernel_width:], blocks[:-1], precision=exact_mode)
    following = jnp.einsum("gij,bigc->bjgc", matrix[:, :, :kernel_width], blocks[1:], precision=exact_mode)
    return (current + following).reshape(-1, padded.shape[1])


def filter_grads(mixed_grad, padded, groups):
    kernel_width = padded.shape[0] - mixed_grad.shape[0]
    grad_blocks = mixed_grad.astype(jnp.float32).reshape(-1, kernel_width, groups, mixed_grad.shape[1] // groups)
    value_blocks = padded.astype(jnp.float32).reshape(-1, kernel_width, groups, mixed_grad.shape[1] // groups)
    earlier = jnp.einsum("bigc,bjgc->gij", grad_blocks, value_blocks[:-1], precision=exact_mode)
    current = jnp.einsum("bigc,bjgc->gij", grad_blocks, value_blocks[1:], precision=exact_mode)
    return lag_sums(jnp.concatenate([earlier, current], axis=2))


def section_grads(layer_input, incoming, short_weights, filters, out_weight):
    tap_count = short_weights.shape[0]
    groups, kernel_width = filters.shape
    channels = layer_input.shape[1]
    weights = short_weights.astype(jnp.float32)
    source = jnp.concatenate([jnp.zeros((tap_count - 1, channels), jnp.float32), layer_input.astype(jnp.float32)], axis=0)
    features = featurize(source, weights)
    products = (features[1] * features[2]).astype(jnp.bfloat16)
    padded = jnp.concatenate([jnp.zeros((kernel_width, channels), jnp.bfloat16), products], axis=0)
    toeplitz = toeplitz_blocks(filters)
    mixed_rows = long_forward(padded, toeplitz, groups)
    gradient = incoming.astype(jnp.float32)
    dense_part = jnp.dot(incoming, jnp.transpose(out_weight), preferred_element_type=jnp.float32).astype(jnp.bfloat16)
    dense_float = dense_part.astype(jnp.float32)
    query_grad = dense_float * mixed_rows
    mixed_grad = (dense_float * features[0]).astype(jnp.bfloat16)
    trailing_grad = jnp.concatenate([mixed_grad, jnp.zeros((kernel_width, channels), jnp.bfloat16)], axis=0)
    product_grad = long_backward(trailing_grad, toeplitz, groups)
    feature_grads = jnp.stack([query_grad, product_grad * features[2], product_grad * features[1]])
    extended = jnp.concatenate([feature_grads, jnp.zeros((3, tap_count - 1, channels), jnp.float32)], axis=1)
    input_grad = (gradient + spread_back(extended, weights)).astype(jnp.bfloat16)
    return input_grad, weight_grads(feature_grads, source), filter_grads(mixed_grad, padded, groups)


def reference(layer_inputs, out_grad, short_weights, long_filters, out_weights):
    sections = layer_inputs.shape[0]
    incoming = out_grad
    input_list = []
    short_list = []
    long_list = []
    for section_index in range(sections - 1, -1, -1):
        input_grad, short_grad, long_grad = section_grads(layer_inputs[section_index], incoming, short_weights[section_index], long_filters[section_index], out_weights[section_index])
        input_list.append(input_grad)
        short_list.append(short_grad)
        long_list.append(long_grad)
        incoming = input_grad
    return jnp.stack(input_list[::-1]), jnp.stack(short_list[::-1]), jnp.stack(long_list[::-1])
```

```python
import functools

import jax
import jax.numpy as jnp
from jax import lax
from jax.experimental import pallas as pl
from jax.experimental.pallas import tpu as pltpu
from jax.sharding import PartitionSpec as P

KL = 128
KS = 7
TILE = 128
GW = 16
AUX = 48
EDGE = 8
PAD = 16
WIN = 2 * KL
BF = jnp.bfloat16
F32 = jnp.float32
VMEM_LIMIT = 60 * 1024 * 1024
INTERPRET = False


def call(body, out_shape, *args, **kwargs):
    return pl.pallas_call(
        body,
        out_shape=out_shape,
        compiler_params=pltpu.CompilerParams(vmem_limit_bytes=VMEM_LIMIT),
        interpret=INTERPRET,
        **kwargs,
    )(*args)


def shape(dims, dtype):
    return jax.ShapeDtypeStruct(dims, dtype)


def dot(a, b):
    return jnp.dot(a, b, preferred_element_type=F32)


def dot_nt(a, b):
    return lax.dot_general(a, b, (((1,), (1,)), ((), ())), preferred_element_type=F32)


def swap_matrix(width):
    size = TILE // width
    n = size * TILE
    row = lax.broadcasted_iota(jnp.int32, (n, n), 0)
    col = lax.broadcasted_iota(jnp.int32, (n, n), 1)
    a, b, j = row // TILE, (row // width) % size, row % width
    return (col == b * TILE + a * width + j).astype(F32).astype(BF)


def split_owned(x, planes, width, matrix):
    step = planes * width
    slices = x.shape[1] // step
    size = TILE // width
    pieces = [[None] * (slices // size) for _ in range(planes)]
    for a in range(slices // size):
        for b in range(planes // size):
            tiles = [
                x[:, (a * size + i) * step + b * TILE : (a * size + i) * step + (b + 1) * TILE]
                for i in range(size)
            ]
            moved = dot(jnp.concatenate(tiles, axis=1), matrix).astype(BF)
            for i in range(size):
                pieces[b * size + i][a] = moved[:, i * TILE : (i + 1) * TILE]
    return [jnp.concatenate(p, axis=1) for p in pieces]


def join_owned(parts, width, matrix):
    planes = len(parts)
    size = TILE // width
    slices = parts[0].shape[1] // width
    out = [[None] * (planes // size) for _ in range(slices)]
    for a in range(slices // size):
        for b in range(planes // size):
            tiles = [parts[b * size + i][:, a * TILE : (a + 1) * TILE] for i in range(size)]
            moved = dot(jnp.concatenate(tiles, axis=1), matrix)
            for i in range(size):
                out[a * size + i][b] = moved[:, i * TILE : (i + 1) * TILE]
    return jnp.concatenate([jnp.concatenate(o, axis=1) for o in out], axis=1)


def filter_rows(slices, planes, per):
    n = slices * planes * per
    row = lax.broadcasted_iota(jnp.int32, (n, n), 0)
    col = lax.broadcasted_iota(jnp.int32, (n, n), 1)
    z, k, g = row // (slices * per), (row // per) % slices, row % per
    return (col == k * planes * per + z * per + g).astype(F32).astype(BF)


def pack_body(planes, slices, width, w_ref, sw_ref, lf_ref, out_ref):
    owned = slices * width
    depth = planes * width
    for z in range(planes):
        block = w_ref[:, z].reshape(owned, depth)
        turned = block.astype(F32).T.astype(BF)
        out_ref[:, z * width : (z + 1) * width, :] = turned.reshape(planes, width, owned)
    base = planes * width
    matrix = swap_matrix(width)
    taps = split_owned(sw_ref[...], planes, width, matrix)
    per = width // GW
    mover = filter_rows(slices, planes, per)
    filters = dot(mover, lf_ref[...]).astype(BF)
    count = slices * per
    zeros = jnp.zeros((GW, owned), BF)
    for z in range(planes):
        out_ref[z, base : base + 32, :] = taps[z]
        out_ref[z, base + 32 : base + AUX, :] = zeros
        out_ref[z, base + 32 : base + 32 + count, :KL] = filters[z * count : (z + 1) * count]


def shuffle_body(planes, halves, width, x_ref, out_ref):
    matrix = swap_matrix(width)
    half = x_ref.shape[1] // halves
    for h in range(halves):
        pieces = split_owned(x_ref[:, h * half : (h + 1) * half], planes, width, matrix)
        for z in range(planes):
            out_ref[z * halves + h] = pieces[z]


def grouped(toeplitz, rows_per, source, groups):
    channels = source.shape[1]
    tiles = []
    for u in range(channels // TILE):
        per = TILE // GW
        full = dot(toeplitz[u * per * rows_per : (u + 1) * per * rows_per], source[:, u * TILE : (u + 1) * TILE])
        lane = lax.broadcasted_iota(jnp.int32, (rows_per, TILE), 1) // GW
        merged = full[:rows_per]
        for g in range(1, per):
            merged = jnp.where(lane == g, full[g * rows_per : (g + 1) * rows_per], merged)
        tiles.append(merged)
    return jnp.concatenate(tiles, axis=1)


def edge_rows(ref, groups):
    return jnp.concatenate(
        [ref[g * KL + KL - PAD : (g + 1) * KL, :] for g in range(groups)], axis=0
    )


def recompute_body(
    groups, own_ref, prev_ref, prev2_ref, next_ref, aux_ref,
    f0_ref, f1_ref, f2_ref, mixed_ref, back_ref, turned_ref,
    rows_ref, band_ref,
):
    rows_ref[0:PAD, :] = prev2_ref[...].astype(F32)
    rows_ref[PAD : PAD + KL, :] = prev_ref[...].astype(F32)
    rows_ref[PAD + KL : PAD + 2 * KL, :] = own_ref[...].astype(F32)
    rows_ref[PAD + 2 * KL :, :] = next_ref[...].astype(F32)
    taps = aux_ref[0:32, :].astype(F32)

    def feature(f, first, count):
        start = PAD + KL + first
        total = taps[f : f + 1] * rows_ref[start : start + count, :]
        for j in range(1, KS):
            total = total + taps[3 * j + f : 3 * j + f + 1] * rows_ref[start - j : start - j + count, :]
        return total

    f0_ref[...] = feature(0, 0, KL)
    key_tail = feature(1, 0, KL + EDGE)
    value_tail = feature(2, 0, KL + EDGE)
    f1_ref[...] = key_tail
    f2_ref[...] = value_tail
    kv = jnp.concatenate([feature(1, -KL, KL) * feature(2, -KL, KL), key_tail * value_tail], axis=0)
    window = kv[:WIN].astype(BF)
    late = kv[EDGE : EDGE + WIN].astype(BF)

    filters = aux_ref[32 : 32 + groups, :KL]
    tap = lax.broadcasted_iota(jnp.int32, (KL, WIN), 0)
    lane = lax.broadcasted_iota(jnp.int32, (KL, WIN), 1)
    ahead = dot(filters, (lane == KL - tap).astype(F32).astype(BF))
    behind = dot(filters, (lane == tap).astype(F32).astype(BF))
    for g in range(groups):
        wide = jnp.broadcast_to(ahead[g : g + 1], (KL, WIN))
        band_ref[g * KL : (g + 1) * KL, :] = pltpu.roll(wide, 0, 1, stride=1, stride_axis=0).astype(BF)
        wide = jnp.broadcast_to(behind[g : g + 1], (KL, WIN))
        back_ref[g * KL : (g + 1) * KL, :] = pltpu.roll(wide, 0, 1, stride=1, stride_axis=0).astype(BF)
    mixed_ref[0:KL, :] = grouped(band_ref, KL, window, groups)
    mixed_ref[KL:, :] = grouped(edge_rows(band_ref, groups), PAD, late, groups)[PAD - EDGE :]
    source = lax.broadcasted_iota(jnp.int32, (WIN, WIN), 0)
    target = lax.broadcasted_iota(jnp.int32, (WIN, WIN), 1)
    mirror = (source + target == WIN - 1).astype(F32).astype(BF)
    turned_ref[...] = dot(mirror, window).astype(BF)


def project_body(tp_ref, own_ref, other_ref, w_ref, out_ref):
    first = tp_ref[0] == 0
    own, other = own_ref[...], other_ref[...]
    low = jnp.where(first, own, other)
    high = jnp.where(first, other, own)
    slices, _, width, owned = w_ref.shape
    half = slices // 2
    total = dot(low, w_ref[:half].reshape(half * width, owned))
    total = total + dot(high, w_ref[half:].reshape(half * width, owned))
    out_ref[0] = total.astype(BF)


def gate_body(parts_ref, f0_ref, send_ref, dgate_ref, early_ref):
    total = parts_ref[0].astype(F32)
    for z in range(1, parts_ref.shape[0]):
        total = total + parts_ref[z].astype(F32)
    dgate = total.astype(BF)
    dmixed = (dgate.astype(F32) * f0_ref[...]).astype(BF)
    send_ref[0:KL, :] = dmixed
    send_ref[KL:, :] = dgate[:PAD]
    dgate_ref[...] = dgate
    early_ref[...] = dmixed[:PAD]


def finish_body(
    groups, send_ref, dgate_ref, near_ref, far_ref, f1_ref, f2_ref, mixed_ref, back_ref, aux_ref, grad_ref,
    out_ref, dkv_ref, d0_ref, d1_ref, d2_ref,
):
    rows = jnp.concatenate(
        [send_ref[0:KL, :], near_ref[0:KL, :], far_ref[...]], axis=0
    )
    window = rows[:WIN]
    late = rows.astype(F32)[EDGE : EDGE + WIN].astype(BF)
    main = grouped(back_ref, KL, window, groups)
    tail = grouped(edge_rows(back_ref, groups), PAD, late, groups)[PAD - EDGE :]
    dkv_ref[...] = main
    d0_ref[0:KL, :] = dgate_ref[...].astype(F32) * mixed_ref[0:KL, :]
    d0_ref[KL:, :] = near_ref[KL:, :].astype(F32)[:EDGE] * mixed_ref[KL:, :]
    d1_ref[0:KL, :] = main * f2_ref[0:KL, :]
    d1_ref[KL:, :] = tail * f2_ref[KL:, :]
    d2_ref[0:KL, :] = main * f1_ref[0:KL, :]
    d2_ref[KL:, :] = tail * f1_ref[KL:, :]
    taps = aux_ref[0:32, :].astype(F32)
    total = grad_ref[...].astype(F32)
    for j in range(KS):
        for f, ref in enumerate((d0_ref, d1_ref, d2_ref)):
            total = total + taps[3 * j + f : 3 * j + f + 1] * ref[j : j + KL, :]
    out_ref[...] = total.astype(BF)


def filters_body(
    groups, dgate_ref, mixed_ref, dkv_ref, f1_ref, f2_ref, own_ref, prev_ref, send_ref, turned_ref,
    out_ref, rows_ref, skew_ref,
):
    channels = own_ref.shape[1]
    rows_ref[0:PAD, :] = prev_ref[KL - PAD :, :].astype(F32)
    rows_ref[PAD:, :] = own_ref[...].astype(F32)
    dkv = dkv_ref[...]
    grads = (
        dgate_ref[...].astype(F32) * mixed_ref[0:KL, :],
        dkv * f2_ref[0:KL, :],
        dkv * f1_ref[0:KL, :],
    )
    sums = []
    for j in range(KS):
        source = rows_ref[PAD - j : PAD - j + KL, :]
        for f in range(3):
            sums.append(jnp.sum(grads[f] * source, axis=0, keepdims=True))
    sums.append(jnp.zeros((32 - 3 * KS, channels), F32))
    out_ref[0:32, :] = jnp.concatenate(sums, axis=0).astype(BF)
    lags = []
    per = TILE // GW
    lane = lax.broadcasted_iota(jnp.int32, (KL, TILE), 1) // GW
    for u in range(channels // TILE):
        grad = send_ref[0:KL, u * TILE : (u + 1) * TILE].astype(F32)
        stacked = jnp.concatenate(
            [jnp.where(lane == g, grad, 0.0).astype(BF) for g in range(per)], axis=0
        )
        skew_ref[...] = dot_nt(stacked, turned_ref[:, u * TILE : (u + 1) * TILE])
        for g in range(per):
            rolled = pltpu.roll(skew_ref[g * KL : (g + 1) * KL, :], 0, 1, stride=1, stride_axis=0)
            lags.append(jnp.sum(rolled, axis=0, keepdims=True))
    if groups < GW:
        lags.append(jnp.zeros((GW - groups, WIN), F32))
    sums = pltpu.roll(jnp.concatenate(lags, axis=0), WIN - (KL - 1), 1)
    out_ref[32:AUX, :] = jnp.zeros((AUX - 32, channels), BF)
    out_ref[32:AUX, :KL] = sums[:, :KL].astype(BF)


def collect_body(width, in_ref, grad_ref, part_ref):
    planes = in_ref.shape[0]
    matrix = swap_matrix(width)
    joined = join_owned([in_ref[z, 0:KL, :] for z in range(planes)], width, matrix)
    grad_ref[...] = joined.astype(BF)
    halves = in_ref.shape[2] // TILE
    for z in range(planes):
        for u in range(halves):
            part_ref[z * halves + u] = in_ref[z, KL:, u * TILE : (u + 1) * TILE]


def sum_body(copies, in_ref, out_ref):
    total = in_ref[0].astype(F32)
    for s in range(1, in_ref.shape[0]):
        total = total + in_ref[s].astype(F32)
    value = total.astype(BF)
    for s in range(copies):
        out_ref[s] = value


def spread_body(planes, slices, width, in_ref, short_ref, long_ref):
    halves = in_ref.shape[0] // planes
    matrix = swap_matrix(width)
    parts = [
        jnp.concatenate([in_ref[z * halves + u, 0:32, :] for u in range(halves)], axis=1)
        for z in range(planes)
    ]
    short_ref[...] = join_owned(parts, width, matrix)
    per = width // GW
    count = slices * per
    stacked = jnp.concatenate(
        [in_ref[z * halves, 32 : 32 + count, :] for z in range(planes)], axis=0
    )
    mover = filter_rows(slices, planes, per)
    long_ref[...] = lax.dot_general(
        mover, stacked, (((0,), (0,)), ((), ())), preferred_element_type=F32
    )


def from_next(x, by):
    size = lax.axis_size("seq")
    return lax.ppermute(x, "seq", [(i, i - by) for i in range(by, size)])


def from_before(x, by):
    size = lax.axis_size("seq")
    return lax.ppermute(x, "seq", [(i, i + by) for i in range(size - by)])


def per_device(layer_inputs, out_grad, short_weights, long_filters, out_weights):
    planes = lax.axis_size("pipe")
    blocks = lax.axis_size("seq")
    depth = out_weights.shape[2]
    half = out_grad.shape[1]
    width = depth // planes
    slices = half // depth
    owned = slices * width
    groups = owned // GW
    tokens = out_grad.shape[0]
    dims = long_filters.shape[1]

    taps = jnp.pad(short_weights[0].reshape(KS * 3, half), ((0, 32 - KS * 3), (0, 0)))
    packed = call(
        functools.partial(pack_body, planes, slices, width),
        shape((planes, planes * width + AUX, owned), BF),
        out_weights[0].reshape(slices, planes, width, depth),
        taps,
        long_filters[0],
    )
    packed = lax.all_to_all(packed, "pipe", 0, 0, tiled=True)
    base = planes * width
    aux = [packed[p, base:] for p in range(planes)]

    def gathered(p):
        whole = lax.all_gather(packed[p, :base], "seq", axis=0)
        return whole.reshape(blocks, planes, width, owned)

    shuffled = call(
        functools.partial(shuffle_body, planes, 2, width),
        shape((planes * 2, layer_inputs.shape[1], owned), BF),
        layer_inputs[0],
    )
    rows = lax.all_to_all(shuffled, ("pipe", "tp"), 0, 0, tiled=True)
    rows = rows.reshape(planes, tokens, owned)
    before = from_before(rows, 1)
    before2 = from_before(rows[:, tokens - PAD :], 2)
    after = from_next(rows[:, :PAD], 1)

    def recomputed(p):
        return call(
            functools.partial(recompute_body, groups),
            (
                shape((KL, owned), F32),
                shape((KL + EDGE, owned), F32),
                shape((KL + EDGE, owned), F32),
                shape((KL + EDGE, owned), F32),
                shape((groups * KL, WIN), BF),
                shape((WIN, owned), BF),
            ),
            rows[p],
            before[p],
            before2[p],
            after[p],
            aux[p],
            scratch_shapes=[
                pltpu.VMEM((2 * KL + 2 * PAD, owned), F32),
                pltpu.VMEM((groups * KL, WIN), BF),
            ],
        )

    tp_index = lax.axis_index("tp").astype(jnp.int32).reshape(1)
    starts = call(
        functools.partial(shuffle_body, planes, 1, width),
        shape((planes, tokens, owned), BF),
        out_grad,
    )
    grad = lax.dynamic_index_in_dim(starts, lax.axis_index("pipe"), 0, keepdims=False)

    outs = [None] * planes
    for p in range(planes - 1, -1, -1):
        weights = gathered(p)
        f0, f1, f2, mixed, back, turned = recomputed(p)
        other = lax.ppermute(grad, "tp", [(0, 1), (1, 0)])
        partial = pl.pallas_call(
            project_body,
            out_shape=shape((planes, tokens, owned), BF),
            grid_spec=pltpu.PrefetchScalarGridSpec(
                num_scalar_prefetch=1,
                grid=(planes,),
                in_specs=[
                    pl.BlockSpec((tokens, owned), lambda z, t: (0, 0)),
                    pl.BlockSpec((tokens, owned), lambda z, t: (0, 0)),
                    pl.BlockSpec((blocks, 1, width, owned), lambda z, t: (0, z, 0, 0)),
                ],
                out_specs=pl.BlockSpec((1, tokens, owned), lambda z, t: (z, 0, 0)),
            ),
            compiler_params=pltpu.CompilerParams(vmem_limit_bytes=VMEM_LIMIT),
            interpret=INTERPRET,
        )(tp_index, grad, other, weights)
        parts = lax.all_to_all(partial, "pipe", 0, 0, tiled=True)
        send, dgate, early = call(
            gate_body,
            (
                shape((KL + PAD, owned), BF),
                shape((KL, owned), BF),
                shape((PAD, owned), BF),
            ),
            parts,
            f0,
        )
        near = from_next(send, 1)
        far = from_next(early, 2)
        new_grad, dkv = call(
            functools.partial(finish_body, groups),
            (shape((KL, owned), BF), shape((KL, owned), F32)),
            send,
            dgate,
            near,
            far,
            f1,
            f2,
            mixed,
            back,
            aux[p],
            grad,
            scratch_shapes=[pltpu.VMEM((KL + EDGE, owned), F32)] * 3,
        )
        filter_grads = call(
            functools.partial(filters_body, groups),
            shape((AUX, owned), BF),
            dgate,
            mixed,
            dkv,
            f1,
            f2,
            rows[p],
            before[p],
            send,
            turned,
            scratch_shapes=[
                pltpu.VMEM((KL + PAD, owned), F32),
                pltpu.VMEM((TILE // GW * KL, WIN), F32),
            ],
        )
        outs[p] = jnp.concatenate([new_grad, filter_grads], axis=0)
        grad = new_grad

    results = lax.all_to_all(jnp.stack(outs), "pipe", 0, 0, tiled=True)
    chunks = planes * owned // TILE
    input_grad, local_sums = call(
        functools.partial(collect_body, width),
        (shape((tokens, half), BF), shape((chunks, AUX, TILE), BF)),
        results,
    )
    exchanged = lax.all_to_all(local_sums, "seq", 0, 0, tiled=True)
    summed = call(
        functools.partial(sum_body, blocks), shape((blocks, AUX, TILE), BF), exchanged
    )
    totals = lax.all_to_all(summed, "seq", 0, 0, tiled=True)
    short_result, long_result = call(
        functools.partial(spread_body, planes, slices, width),
        (shape((32, half), F32), shape((dims, KL), F32)),
        totals,
    )
    short_result = short_result[: KS * 3].reshape(1, KS, 3, half)
    return input_grad[None], short_result, long_result[None]


def solution(mesh):
    in_specs = (
        P("pipe", ("seq", "tp"), None),
        P("seq", "tp"),
        P("pipe", None, None, "tp"),
        P("pipe", "tp", None),
        P("pipe", "tp", "seq"),
    )
    out_specs = (P("pipe", "seq", "tp"), P("pipe", None, None, "tp"), P("pipe", "tp", None))
    return jax.shard_map(
        per_device, mesh=mesh, in_specs=in_specs, out_specs=out_specs, check_vma=False
    )
```

```python
import functools

import jax
import jax.numpy as jnp
from jax import lax
from jax.experimental import pallas as pl
from jax.experimental.pallas import tpu as pltpu
from jax.sharding import PartitionSpec as P

KL = 128
KS = 7
TILE = 128
GW = 16
AUX = 48
EDGE = 8
PAD = 16
WIN = 2 * KL
BF = jnp.bfloat16
F32 = jnp.float32
VMEM_LIMIT = 60 * 1024 * 1024
INTERPRET = False


def call(body, out_shape, *args, **kwargs):
    return pl.pallas_call(
        body,
        out_shape=out_shape,
        compiler_params=pltpu.CompilerParams(vmem_limit_bytes=VMEM_LIMIT),
        interpret=INTERPRET,
        **kwargs,
    )(*args)


def shape(dims, dtype):
    return jax.ShapeDtypeStruct(dims, dtype)


def dot(a, b):
    return jnp.dot(a, b, preferred_element_type=F32)


def dot_nt(a, b):
    return lax.dot_general(a, b, (((1,), (1,)), ((), ())), preferred_element_type=F32)


def swap_matrix(width):
    size = TILE // width
    n = size * TILE
    row = lax.broadcasted_iota(jnp.int32, (n, n), 0)
    col = lax.broadcasted_iota(jnp.int32, (n, n), 1)
    a, b, j = row // TILE, (row // width) % size, row % width
    return (col == b * TILE + a * width + j).astype(F32).astype(BF)


def split_owned(x, planes, width, matrix):
    step = planes * width
    slices = x.shape[1] // step
    size = TILE // width
    pieces = [[None] * (slices // size) for _ in range(planes)]
    for a in range(slices // size):
        for b in range(planes // size):
            tiles = [
                x[:, (a * size + i) * step + b * TILE : (a * size + i) * step + (b + 1) * TILE]
                for i in range(size)
            ]
            moved = dot(jnp.concatenate(tiles, axis=1), matrix).astype(BF)
            for i in range(size):
                pieces[b * size + i][a] = moved[:, i * TILE : (i + 1) * TILE]
    return [jnp.concatenate(p, axis=1) for p in pieces]


def join_owned(parts, width, matrix):
    planes = len(parts)
    size = TILE // width
    slices = parts[0].shape[1] // width
    out = [[None] * (planes // size) for _ in range(slices)]
    for a in range(slices // size):
        for b in range(planes // size):
            tiles = [parts[b * size + i][:, a * TILE : (a + 1) * TILE] for i in range(size)]
            moved = dot(jnp.concatenate(tiles, axis=1), matrix)
            for i in range(size):
                out[a * size + i][b] = moved[:, i * TILE : (i + 1) * TILE]
    return jnp.concatenate([jnp.concatenate(o, axis=1) for o in out], axis=1)


def filter_rows(slices, planes, per):
    n = slices * planes * per
    row = lax.broadcasted_iota(jnp.int32, (n, n), 0)
    col = lax.broadcasted_iota(jnp.int32, (n, n), 1)
    z, k, g = row // (slices * per), (row // per) % slices, row % per
    return (col == k * planes * per + z * per + g).astype(F32).astype(BF)


def pack_body(planes, slices, width, tp_ref, w_ref, sw_ref, lf_ref, x_ref, other_ref, out_ref):
    owned = slices * width
    depth = planes * width
    half = slices * depth
    count = x_ref.shape[0]
    matrix = swap_matrix(width)
    tp = tp_ref[0]
    start = pl.multiple_of(tp * half, TILE)
    for source, place in ((x_ref, tp), (other_ref, 1 - tp)):
        pieces = split_owned(source[:, pl.ds(start, half)], planes, width, matrix)
        at = pl.multiple_of(place * count, PAD)
        for z in range(planes):
            out_ref[z, pl.ds(at, count), :] = pieces[z]
    for z in range(planes):
        block = w_ref[:, z].reshape(owned, depth)
        turned = block.astype(F32).T.astype(BF)
        low = KL + z * width
        out_ref[:, low : low + width, :] = turned.reshape(planes, width, owned)
    base = KL + depth
    taps = [sw_ref[j].astype(F32) for j in range(KS)]
    taps.append(jnp.zeros((32 - 3 * KS, half), F32))
    taps = split_owned(jnp.concatenate(taps, axis=0).astype(BF), planes, width, matrix)
    per = width // GW
    filters = dot(filter_rows(slices, planes, per), lf_ref[...]).astype(BF)
    groups = slices * per
    for z in range(planes):
        out_ref[z, base : base + 32, :] = taps[z]
        out_ref[z, base + 32 : base + AUX, :] = jnp.zeros((GW, owned), BF)
        out_ref[z, base + 32 : base + 32 + groups, :KL] = filters[z * groups : (z + 1) * groups]


def shuffle_body(planes, width, x_ref, out_ref):
    pieces = split_owned(x_ref[...], planes, width, swap_matrix(width))
    for z in range(planes):
        out_ref[z] = pieces[z]


def grouped(toeplitz, rows_per, source, groups):
    channels = source.shape[1]
    tiles = []
    for u in range(channels // TILE):
        per = TILE // GW
        full = dot(toeplitz[u * per * rows_per : (u + 1) * per * rows_per], source[:, u * TILE : (u + 1) * TILE])
        lane = lax.broadcasted_iota(jnp.int32, (rows_per, TILE), 1) // GW
        merged = full[:rows_per]
        for g in range(1, per):
            merged = jnp.where(lane == g, full[g * rows_per : (g + 1) * rows_per], merged)
        tiles.append(merged)
    return jnp.concatenate(tiles, axis=1)


def edge_rows(ref, groups):
    return jnp.concatenate(
        [ref[g * KL + KL - PAD : (g + 1) * KL, :] for g in range(groups)], axis=0
    )


def recompute_body(
    groups, own_ref, prev_ref, prev2_ref, next_ref, aux_ref,
    f0_ref, f1_ref, f2_ref, mixed_ref, back_ref, turned_ref,
    rows_ref, band_ref,
):
    rows_ref[0:PAD, :] = prev2_ref[...].astype(F32)
    rows_ref[PAD : PAD + KL, :] = prev_ref[...].astype(F32)
    rows_ref[PAD + KL : PAD + 2 * KL, :] = own_ref[...].astype(F32)
    rows_ref[PAD + 2 * KL :, :] = next_ref[...].astype(F32)
    taps = aux_ref[0:32, :].astype(F32)

    def feature(f, first, count):
        start = PAD + KL + first
        total = taps[f : f + 1] * rows_ref[start : start + count, :]
        for j in range(1, KS):
            total = total + taps[3 * j + f : 3 * j + f + 1] * rows_ref[start - j : start - j + count, :]
        return total

    f0_ref[...] = feature(0, 0, KL)
    key_tail = feature(1, 0, KL + EDGE)
    value_tail = feature(2, 0, KL + EDGE)
    f1_ref[...] = key_tail
    f2_ref[...] = value_tail
    kv = jnp.concatenate([feature(1, -KL, KL) * feature(2, -KL, KL), key_tail * value_tail], axis=0)
    window = kv[:WIN].astype(BF)
    late = kv[EDGE : EDGE + WIN].astype(BF)

    filters = aux_ref[32 : 32 + groups, :KL]
    tap = lax.broadcasted_iota(jnp.int32, (KL, WIN), 0)
    lane = lax.broadcasted_iota(jnp.int32, (KL, WIN), 1)
    ahead = dot(filters, (lane == KL - tap).astype(F32).astype(BF))
    behind = dot(filters, (lane == tap).astype(F32).astype(BF))
    for g in range(groups):
        wide = jnp.broadcast_to(ahead[g : g + 1], (KL, WIN))
        band_ref[g * KL : (g + 1) * KL, :] = pltpu.roll(wide, 0, 1, stride=1, stride_axis=0).astype(BF)
        wide = jnp.broadcast_to(behind[g : g + 1], (KL, WIN))
        back_ref[g * KL : (g + 1) * KL, :] = pltpu.roll(wide, 0, 1, stride=1, stride_axis=0).astype(BF)
    mixed_ref[0:KL, :] = grouped(band_ref, KL, window, groups)
    mixed_ref[KL:, :] = grouped(edge_rows(band_ref, groups), PAD, late, groups)[PAD - EDGE :]
    source = lax.broadcasted_iota(jnp.int32, (WIN, WIN), 0)
    target = lax.broadcasted_iota(jnp.int32, (WIN, WIN), 1)
    mirror = (source + target == WIN - 1).astype(F32).astype(BF)
    turned_ref[...] = dot(mirror, window).astype(BF)


def project_body(tp_ref, own_ref, other_ref, w_ref, out_ref):
    first = tp_ref[0] == 0
    own, other = own_ref[...], other_ref[...]
    rows = jnp.concatenate([jnp.where(first, own, other), jnp.where(first, other, own)], axis=1)
    slices, _, count, width, owned = w_ref.shape
    for z in range(count):
        out_ref[z] = dot(rows, w_ref[:, 0, z].reshape(slices * width, owned)).astype(BF)


def gate_body(parts_ref, f0_ref, send_ref, dgate_ref, early_ref):
    total = parts_ref[0].astype(F32)
    for z in range(1, parts_ref.shape[0]):
        total = total + parts_ref[z].astype(F32)
    dgate = total.astype(BF)
    dmixed = (dgate.astype(F32) * f0_ref[...]).astype(BF)
    send_ref[0:KL, :] = dmixed
    send_ref[KL:, :] = dgate[:PAD]
    dgate_ref[...] = dgate
    early_ref[...] = dmixed[:PAD]


def finish_body(
    groups, send_ref, dgate_ref, near_ref, far_ref, f1_ref, f2_ref, mixed_ref, back_ref, aux_ref, grad_ref,
    out_ref, dkv_ref, d0_ref, d1_ref, d2_ref,
):
    rows = jnp.concatenate(
        [send_ref[0:KL, :], near_ref[0:KL, :], far_ref[...]], axis=0
    )
    window = rows[:WIN]
    late = rows.astype(F32)[EDGE : EDGE + WIN].astype(BF)
    main = grouped(back_ref, KL, window, groups)
    tail = grouped(edge_rows(back_ref, groups), PAD, late, groups)[PAD - EDGE :]
    dkv_ref[...] = main
    d0_ref[0:KL, :] = dgate_ref[...].astype(F32) * mixed_ref[0:KL, :]
    d0_ref[KL:, :] = near_ref[KL:, :].astype(F32)[:EDGE] * mixed_ref[KL:, :]
    d1_ref[0:KL, :] = main * f2_ref[0:KL, :]
    d1_ref[KL:, :] = tail * f2_ref[KL:, :]
    d2_ref[0:KL, :] = main * f1_ref[0:KL, :]
    d2_ref[KL:, :] = tail * f1_ref[KL:, :]
    taps = aux_ref[0:32, :].astype(F32)
    total = grad_ref[...].astype(F32)
    for j in range(KS):
        for f, ref in enumerate((d0_ref, d1_ref, d2_ref)):
            total = total + taps[3 * j + f : 3 * j + f + 1] * ref[j : j + KL, :]
    out_ref[...] = total.astype(BF)


def filters_body(
    groups, dgate_ref, mixed_ref, dkv_ref, f1_ref, f2_ref, own_ref, prev_ref, send_ref, turned_ref,
    *refs,
):
    out_ref, rows_ref, skew_ref = refs[-3:]
    channels = own_ref.shape[1]
    rows_ref[0:PAD, :] = prev_ref[KL - PAD :, :].astype(F32)
    rows_ref[PAD:, :] = own_ref[...].astype(F32)
    dkv = dkv_ref[...]
    grads = (
        dgate_ref[...].astype(F32) * mixed_ref[0:KL, :],
        dkv * f2_ref[0:KL, :],
        dkv * f1_ref[0:KL, :],
    )
    sums = []
    for j in range(KS):
        source = rows_ref[PAD - j : PAD - j + KL, :]
        for f in range(3):
            sums.append(jnp.sum(grads[f] * source, axis=0, keepdims=True))
    sums.append(jnp.zeros((32 - 3 * KS, channels), F32))
    short = jnp.concatenate(sums, axis=0).astype(BF)
    for u in range(channels // TILE):
        out_ref[u, 0:32, :] = short[:, u * TILE : (u + 1) * TILE]
    lags = []
    per = TILE // GW
    lane = lax.broadcasted_iota(jnp.int32, (KL, TILE), 1) // GW
    for u in range(channels // TILE):
        grad = send_ref[0:KL, u * TILE : (u + 1) * TILE].astype(F32)
        stacked = jnp.concatenate(
            [jnp.where(lane == g, grad, 0.0).astype(BF) for g in range(per)], axis=0
        )
        skew_ref[...] = dot_nt(stacked, turned_ref[:, u * TILE : (u + 1) * TILE])
        for g in range(per):
            rolled = pltpu.roll(skew_ref[g * KL : (g + 1) * KL, :], 0, 1, stride=1, stride_axis=0)
            lags.append(jnp.sum(rolled, axis=0, keepdims=True))
    if groups < GW:
        lags.append(jnp.zeros((GW - groups, WIN), F32))
    sums = pltpu.roll(jnp.concatenate(lags, axis=0), WIN - (KL - 1), 1)
    long = sums[:, :KL].astype(BF)
    for u in range(channels // TILE):
        out_ref[u, 32:AUX, :] = long


def sum_body(copies, in_ref, out_ref):
    total = in_ref[0].astype(F32)
    for s in range(1, in_ref.shape[0]):
        total = total + in_ref[s].astype(F32)
    value = total.astype(BF)
    for s in range(copies):
        out_ref[s] = value


def merge_body(sums_ref, *refs):
    grads, out_ref = refs[:-1], refs[-1]
    halves = sums_ref.shape[0] // len(grads)
    for p, ref in enumerate(grads):
        out_ref[p, :KL, :] = ref[...]
        for u in range(halves):
            out_ref[p, KL:, u * TILE : (u + 1) * TILE] = sums_ref[p * halves + u]


def spread_body(slices, width, in_ref, grad_ref, short_ref, long_ref):
    planes = in_ref.shape[0]
    matrix = swap_matrix(width)
    grad_ref[...] = join_owned([in_ref[z, :KL] for z in range(planes)], width, matrix).astype(BF)
    short = join_owned([in_ref[z, KL : KL + 32] for z in range(planes)], width, matrix)
    for j in range(KS):
        short_ref[j] = short[3 * j : 3 * j + 3]
    per = width // GW
    groups = slices * per
    stacked = jnp.concatenate(
        [in_ref[z, KL + 32 : KL + 32 + groups, :KL] for z in range(planes)], axis=0
    )
    mover = filter_rows(slices, planes, per)
    long_ref[...] = lax.dot_general(
        mover, stacked, (((0,), (0,)), ((), ())), preferred_element_type=F32
    )


def from_next(x, by):
    size = lax.axis_size("seq")
    return lax.ppermute(x, "seq", [(i, i - by) for i in range(by, size)])


def from_before(x, by):
    size = lax.axis_size("seq")
    return lax.ppermute(x, "seq", [(i, i + by) for i in range(size - by)])


def per_device(layer_inputs, out_grad, short_weights, long_filters, out_weights):
    planes = lax.axis_size("pipe")
    blocks = lax.axis_size("seq")
    depth = out_weights.shape[2]
    half = out_grad.shape[1]
    width = depth // planes
    slices = half // depth
    owned = slices * width
    groups = owned // GW
    tokens = out_grad.shape[0]
    dims = long_filters.shape[1]

    tp_index = lax.axis_index("tp").astype(jnp.int32).reshape(1)
    own_rows = layer_inputs[0]
    swapped = lax.ppermute(own_rows, "tp", [(0, 1), (1, 0)])
    packed = pl.pallas_call(
        functools.partial(pack_body, planes, slices, width),
        out_shape=shape((planes, tokens + depth + AUX, owned), BF),
        in_specs=[pl.BlockSpec(memory_space=pltpu.SMEM)]
        + [pl.BlockSpec(memory_space=pltpu.VMEM)] * 5,
        compiler_params=pltpu.CompilerParams(vmem_limit_bytes=VMEM_LIMIT),
        interpret=INTERPRET,
    )(
        tp_index,
        out_weights[0].reshape(slices, planes, width, depth),
        short_weights[0],
        long_filters[0],
        own_rows,
        swapped,
    )
    packed = lax.all_to_all(packed, "pipe", 0, 0, tiled=True)
    rows = packed[:, :tokens]
    before = from_before(rows, 1)
    before2 = from_before(rows[:, tokens - PAD :], 2)
    after = from_next(rows[:, :PAD], 1)

    def whole(x):
        return pl.BlockSpec(x.shape, lambda i: (0,) * len(x.shape))

    def plane(x, p, count, at=0):
        return pl.BlockSpec((None, count, x.shape[2]), lambda i, p=p, at=at: (p, at, 0))

    def own_block(p):
        return plane(packed, p, tokens)

    def aux_block(p):
        return plane(packed, p, AUX, (tokens + depth) // AUX)

    def gathered(first, last):
        pieces = lax.all_gather(packed[first : last + 1, tokens : tokens + depth], "seq", axis=0)
        return pieces.reshape(blocks, last + 1 - first, planes, width, owned)

    def copied(p):
        copies = jnp.broadcast_to(packed[p, tokens : tokens + depth][None], (blocks, depth, owned))
        pieces = lax.all_to_all(copies, "seq", 0, 0, tiled=True)
        return pieces.reshape(blocks, 1, planes, width, owned)

    weights = {planes - 1: (copied(planes - 1), 0)}
    last = planes - 2
    for size in (2, 2, planes):
        first = max(0, last - size + 1)
        if last >= first:
            group = gathered(first, last)
            weights.update({p: (group, p - first) for p in range(first, last + 1)})
        last = first - 1

    def recomputed(p):
        results = (
            shape((KL, owned), F32),
            shape((KL + EDGE, owned), F32),
            shape((KL + EDGE, owned), F32),
            shape((KL + EDGE, owned), F32),
            shape((groups * KL, WIN), BF),
            shape((WIN, owned), BF),
        )
        return call(
            functools.partial(recompute_body, groups),
            results,
            packed,
            before,
            before2,
            after,
            packed,
            grid=(1,),
            in_specs=[
                own_block(p),
                plane(before, p, tokens),
                plane(before2, p, PAD),
                plane(after, p, PAD),
                aux_block(p),
            ],
            out_specs=tuple(whole(r) for r in results),
            scratch_shapes=[
                pltpu.VMEM((2 * KL + 2 * PAD, owned), F32),
                pltpu.VMEM((groups * KL, WIN), BF),
            ],
        )

    starts = call(
        functools.partial(shuffle_body, planes, width),
        shape((planes, tokens, owned), BF),
        out_grad,
    )
    grad = lax.dynamic_index_in_dim(starts, lax.axis_index("pipe"), 0, keepdims=False)

    outs = [None] * planes
    sums = None
    for p in range(planes - 1, -1, -1):
        group, at = weights[p]
        f0, f1, f2, mixed, back, turned = recomputed(p)
        if p == planes - 1:
            group, f0, f1, f2, mixed, back, turned = lax.optimization_barrier(
                (group, f0, f1, f2, mixed, back, turned)
            )
        other = lax.ppermute(grad, "tp", [(0, 1), (1, 0)])
        partial = pl.pallas_call(
            project_body,
            out_shape=shape((planes, tokens, owned), BF),
            grid_spec=pltpu.PrefetchScalarGridSpec(
                num_scalar_prefetch=1,
                grid=(2,),
                in_specs=[
                    pl.BlockSpec((tokens, owned), lambda z, t: (0, 0)),
                    pl.BlockSpec((tokens, owned), lambda z, t: (0, 0)),
                    pl.BlockSpec(
                        (blocks, 1, planes // 2, width, owned), lambda z, t, at=at: (0, at, z, 0, 0)
                    ),
                ],
                out_specs=pl.BlockSpec((planes // 2, tokens, owned), lambda z, t: (z, 0, 0)),
            ),
            compiler_params=pltpu.CompilerParams(vmem_limit_bytes=VMEM_LIMIT),
            interpret=INTERPRET,
        )(tp_index, grad, other, group)
        parts = lax.all_to_all(partial, "pipe", 0, 0, tiled=True)
        if sums is not None:
            parts, sums = lax.optimization_barrier((parts, sums))
        send, dgate, early = call(
            gate_body,
            (
                shape((KL + PAD, owned), BF),
                shape((KL, owned), BF),
                shape((PAD, owned), BF),
            ),
            parts,
            f0,
        )
        near = from_next(send, 1)
        far = from_next(early, 2)
        results = (shape((KL, owned), BF), shape((KL, owned), F32))
        operands = (send, dgate, near, far, f1, f2, mixed, back, packed, grad)
        new_grad, dkv = call(
            functools.partial(finish_body, groups),
            results,
            *operands,
            grid=(1,),
            in_specs=[aux_block(p) if x is packed else whole(x) for x in operands],
            out_specs=tuple(whole(r) for r in results),
            scratch_shapes=[pltpu.VMEM((KL + EDGE, owned), F32)] * 3,
        )
        halves = owned // TILE
        result = shape((planes * halves, AUX, TILE), BF)
        operands = [dgate, mixed, dkv, f1, f2, packed, before, send, turned]
        specs = [whole(x) for x in operands]
        specs[5:7] = [own_block(p), plane(before, p, tokens)]
        aliases = {}
        if sums is not None:
            aliases = {len(operands): 0}
            operands.append(sums)
            specs.append(pl.BlockSpec(memory_space=pl.ANY))
        sums = call(
            functools.partial(filters_body, groups),
            result,
            *operands,
            grid=(1,),
            in_specs=specs,
            out_specs=pl.BlockSpec((halves, AUX, TILE), lambda i, p=p: (p, 0, 0)),
            input_output_aliases=aliases,
            scratch_shapes=[
                pltpu.VMEM((KL + PAD, owned), F32),
                pltpu.VMEM((TILE // GW * KL, WIN), F32),
            ],
        )
        outs[p] = new_grad
        grad = new_grad

    exchanged = lax.all_to_all(sums, "seq", 0, 0, tiled=True)
    summed = call(
        functools.partial(sum_body, blocks), shape((blocks, AUX, TILE), BF), exchanged
    )
    summed = lax.all_to_all(summed, "seq", 0, 0, tiled=True)
    merged = call(merge_body, shape((planes, tokens + AUX, owned), BF), summed, *outs)
    results = lax.all_to_all(merged, "pipe", 0, 0, tiled=True)
    input_grad, short_result, long_result = call(
        functools.partial(spread_body, slices, width),
        (shape((tokens, half), BF), shape((KS, 3, half), F32), shape((dims, KL), F32)),
        results,
    )
    return input_grad[None], short_result[None], long_result[None]


def solution(mesh):
    in_specs = (
        P("pipe", ("seq", "tp"), None),
        P("seq", "tp"),
        P("pipe", None, None, "tp"),
        P("pipe", "tp", None),
        P("pipe", "tp", "seq"),
    )
    out_specs = (P("pipe", "seq", "tp"), P("pipe", None, None, "tp"), P("pipe", "tp", None))
    return jax.shard_map(
        per_device, mesh=mesh, in_specs=in_specs, out_specs=out_specs, check_vma=False
    )
```

```python
import functools

import jax
import jax.numpy as jnp
from jax import lax
from jax.experimental import pallas as pl
from jax.experimental.pallas import tpu as pltpu
from jax.sharding import PartitionSpec as P

KL = 128
KS = 7
TILE = 128
GW = 16
AUX = 48
EDGE = 8
PAD = 16
WIN = 2 * KL
BF = jnp.bfloat16
F32 = jnp.float32
VMEM_LIMIT = 24 * 1024 * 1024
INTERPRET = False


def call(body, out_shape, *args, **kwargs):
    return pl.pallas_call(
        body,
        out_shape=out_shape,
        compiler_params=pltpu.CompilerParams(vmem_limit_bytes=VMEM_LIMIT),
        interpret=INTERPRET,
        **kwargs,
    )(*args)


def shape(dims, dtype):
    return jax.ShapeDtypeStruct(dims, dtype)


def dot(a, b):
    return jnp.dot(a, b, preferred_element_type=F32)


def dot_nt(a, b):
    return lax.dot_general(a, b, (((1,), (1,)), ((), ())), preferred_element_type=F32)


def swap_matrix(width):
    size = TILE // width
    n = size * TILE
    row = lax.broadcasted_iota(jnp.int32, (n, n), 0)
    col = lax.broadcasted_iota(jnp.int32, (n, n), 1)
    a, b, j = row // TILE, (row // width) % size, row % width
    return (col == b * TILE + a * width + j).astype(F32).astype(BF)


def split_owned(x, planes, width, matrix):
    step = planes * width
    slices = x.shape[1] // step
    size = TILE // width
    pieces = [[None] * (slices // size) for _ in range(planes)]
    for a in range(slices // size):
        for b in range(planes // size):
            tiles = [
                x[:, (a * size + i) * step + b * TILE : (a * size + i) * step + (b + 1) * TILE]
                for i in range(size)
            ]
            moved = dot(jnp.concatenate(tiles, axis=1), matrix).astype(BF)
            for i in range(size):
                pieces[b * size + i][a] = moved[:, i * TILE : (i + 1) * TILE]
    return [jnp.concatenate(p, axis=1) for p in pieces]


def join_owned(parts, width, matrix):
    planes = len(parts)
    size = TILE // width
    slices = parts[0].shape[1] // width
    out = [[None] * (planes // size) for _ in range(slices)]
    for a in range(slices // size):
        for b in range(planes // size):
            tiles = [parts[b * size + i][:, a * TILE : (a + 1) * TILE] for i in range(size)]
            moved = dot(jnp.concatenate(tiles, axis=1), matrix)
            for i in range(size):
                out[a * size + i][b] = moved[:, i * TILE : (i + 1) * TILE]
    return jnp.concatenate([jnp.concatenate(o, axis=1) for o in out], axis=1)


def filter_rows(slices, planes, per):
    n = slices * planes * per
    row = lax.broadcasted_iota(jnp.int32, (n, n), 0)
    col = lax.broadcasted_iota(jnp.int32, (n, n), 1)
    z, k, g = row // (slices * per), (row // per) % slices, row % per
    return (col == k * planes * per + z * per + g).astype(F32).astype(BF)


def pack_body(planes, slices, width, tp_ref, w_ref, sw_ref, lf_ref, x_ref, other_ref, out_ref):
    owned = slices * width
    depth = planes * width
    half = slices * depth
    count = x_ref.shape[0]
    matrix = swap_matrix(width)
    tp = tp_ref[0]
    start = pl.multiple_of(tp * half, TILE)
    for source, place in ((x_ref, tp), (other_ref, 1 - tp)):
        pieces = split_owned(source[:, pl.ds(start, half)], planes, width, matrix)
        at = pl.multiple_of(place * count, PAD)
        for z in range(planes):
            out_ref[z, pl.ds(at, count), :] = pieces[z]
    for z in range(planes):
        block = w_ref[:, z].reshape(owned, depth)
        turned = block.astype(F32).T.astype(BF)
        low = KL + z * width
        out_ref[:, low : low + width, :] = turned.reshape(planes, width, owned)
    base = KL + depth
    taps = [sw_ref[j].astype(F32) for j in range(KS)]
    taps.append(jnp.zeros((32 - 3 * KS, half), F32))
    taps = split_owned(jnp.concatenate(taps, axis=0).astype(BF), planes, width, matrix)
    per = width // GW
    filters = dot(filter_rows(slices, planes, per), lf_ref[...]).astype(BF)
    groups = slices * per
    for z in range(planes):
        out_ref[z, base : base + 32, :] = taps[z]
        out_ref[z, base + 32 : base + AUX, :] = jnp.zeros((GW, owned), BF)
        out_ref[z, base + 32 : base + 32 + groups, :KL] = filters[z * groups : (z + 1) * groups]


def shuffle_body(planes, width, x_ref, out_ref):
    pieces = split_owned(x_ref[...], planes, width, swap_matrix(width))
    for z in range(planes):
        out_ref[z] = pieces[z]


def grouped(toeplitz, rows_per, source, groups):
    channels = source.shape[1]
    tiles = []
    for u in range(channels // TILE):
        per = TILE // GW
        full = dot(toeplitz[u * per * rows_per : (u + 1) * per * rows_per], source[:, u * TILE : (u + 1) * TILE])
        lane = lax.broadcasted_iota(jnp.int32, (rows_per, TILE), 1) // GW
        merged = full[:rows_per]
        for g in range(1, per):
            merged = jnp.where(lane == g, full[g * rows_per : (g + 1) * rows_per], merged)
        tiles.append(merged)
    return jnp.concatenate(tiles, axis=1)


def edge_rows(ref, groups):
    return jnp.concatenate(
        [ref[g * KL + KL - PAD : (g + 1) * KL, :] for g in range(groups)], axis=0
    )


def recompute_body(
    groups, own_ref, prev_ref, prev2_ref, next_ref, aux_ref,
    f0_ref, f1_ref, f2_ref, mixed_ref, back_ref, turned_ref,
    rows_ref, band_ref,
):
    rows_ref[0:PAD, :] = prev2_ref[...].astype(F32)
    rows_ref[PAD : PAD + KL, :] = prev_ref[...].astype(F32)
    rows_ref[PAD + KL : PAD + 2 * KL, :] = own_ref[...].astype(F32)
    rows_ref[PAD + 2 * KL :, :] = next_ref[...].astype(F32)
    taps = aux_ref[0:32, :].astype(F32)

    def feature(f, first, count):
        start = PAD + KL + first
        total = taps[f : f + 1] * rows_ref[start : start + count, :]
        for j in range(1, KS):
            total = total + taps[3 * j + f : 3 * j + f + 1] * rows_ref[start - j : start - j + count, :]
        return total

    f0_ref[...] = feature(0, 0, KL)
    key_tail = feature(1, 0, KL + EDGE)
    value_tail = feature(2, 0, KL + EDGE)
    f1_ref[...] = key_tail
    f2_ref[...] = value_tail
    kv = jnp.concatenate([feature(1, -KL, KL) * feature(2, -KL, KL), key_tail * value_tail], axis=0)
    window = kv[:WIN].astype(BF)
    late = kv[EDGE : EDGE + WIN].astype(BF)

    filters = aux_ref[32 : 32 + groups, :KL]
    tap = lax.broadcasted_iota(jnp.int32, (KL, WIN), 0)
    lane = lax.broadcasted_iota(jnp.int32, (KL, WIN), 1)
    ahead = dot(filters, (lane == KL - tap).astype(F32).astype(BF))
    behind = dot(filters, (lane == tap).astype(F32).astype(BF))
    for g in range(groups):
        wide = jnp.broadcast_to(ahead[g : g + 1], (KL, WIN))
        band_ref[g * KL : (g + 1) * KL, :] = pltpu.roll(wide, 0, 1, stride=1, stride_axis=0).astype(BF)
        wide = jnp.broadcast_to(behind[g : g + 1], (KL, WIN))
        back_ref[g * KL : (g + 1) * KL, :] = pltpu.roll(wide, 0, 1, stride=1, stride_axis=0).astype(BF)
    mixed_ref[0:KL, :] = grouped(band_ref, KL, window, groups)
    mixed_ref[KL:, :] = grouped(edge_rows(band_ref, groups), PAD, late, groups)[PAD - EDGE :]
    source = lax.broadcasted_iota(jnp.int32, (WIN, WIN), 0)
    target = lax.broadcasted_iota(jnp.int32, (WIN, WIN), 1)
    mirror = (source + target == WIN - 1).astype(F32).astype(BF)
    turned_ref[...] = dot(mirror, window).astype(BF)


def project_body(tp_ref, own_ref, other_ref, w_ref, out_ref):
    first = tp_ref[0] == 0
    own, other = own_ref[...], other_ref[...]
    rows = jnp.concatenate([jnp.where(first, own, other), jnp.where(first, other, own)], axis=1)
    slices, _, count, width, owned = w_ref.shape
    for z in range(count):
        out_ref[z] = dot(rows, w_ref[:, 0, z].reshape(slices * width, owned)).astype(BF)


def gate_body(parts_ref, f0_ref, send_ref, dgate_ref, early_ref):
    total = parts_ref[0].astype(F32)
    for z in range(1, parts_ref.shape[0]):
        total = total + parts_ref[z].astype(F32)
    dgate = total.astype(BF)
    dmixed = (dgate.astype(F32) * f0_ref[...]).astype(BF)
    send_ref[0:KL, :] = dmixed
    send_ref[KL:, :] = dgate[:PAD]
    dgate_ref[...] = dgate
    early_ref[...] = dmixed[:PAD]


def finish_body(
    groups, send_ref, dgate_ref, near_ref, far_ref, f1_ref, f2_ref, mixed_ref, back_ref, aux_ref, grad_ref,
    out_ref, dkv_ref, d0_ref, d1_ref, d2_ref,
):
    rows = jnp.concatenate(
        [send_ref[0:KL, :], near_ref[0:KL, :], far_ref[...]], axis=0
    )
    window = rows[:WIN]
    late = rows.astype(F32)[EDGE : EDGE + WIN].astype(BF)
    main = grouped(back_ref, KL, window, groups)
    tail = grouped(edge_rows(back_ref, groups), PAD, late, groups)[PAD - EDGE :]
    dkv_ref[...] = main
    d0_ref[0:KL, :] = dgate_ref[...].astype(F32) * mixed_ref[0:KL, :]
    d0_ref[KL:, :] = near_ref[KL:, :].astype(F32)[:EDGE] * mixed_ref[KL:, :]
    d1_ref[0:KL, :] = main * f2_ref[0:KL, :]
    d1_ref[KL:, :] = tail * f2_ref[KL:, :]
    d2_ref[0:KL, :] = main * f1_ref[0:KL, :]
    d2_ref[KL:, :] = tail * f1_ref[KL:, :]
    taps = aux_ref[0:32, :].astype(F32)
    total = grad_ref[...].astype(F32)
    for j in range(KS):
        for f, ref in enumerate((d0_ref, d1_ref, d2_ref)):
            total = total + taps[3 * j + f : 3 * j + f + 1] * ref[j : j + KL, :]
    out_ref[...] = total.astype(BF)


def filters_body(
    groups, dgate_ref, mixed_ref, dkv_ref, f1_ref, f2_ref, own_ref, prev_ref, send_ref, turned_ref,
    *refs,
):
    out_ref, rows_ref, skew_ref = refs[-3:]
    channels = own_ref.shape[1]
    rows_ref[0:PAD, :] = prev_ref[KL - PAD :, :].astype(F32)
    rows_ref[PAD:, :] = own_ref[...].astype(F32)
    dkv = dkv_ref[...]
    grads = (
        dgate_ref[...].astype(F32) * mixed_ref[0:KL, :],
        dkv * f2_ref[0:KL, :],
        dkv * f1_ref[0:KL, :],
    )
    sums = []
    for j in range(KS):
        source = rows_ref[PAD - j : PAD - j + KL, :]
        for f in range(3):
            sums.append(jnp.sum(grads[f] * source, axis=0, keepdims=True))
    sums.append(jnp.zeros((32 - 3 * KS, channels), F32))
    short = jnp.concatenate(sums, axis=0).astype(BF)
    for u in range(channels // TILE):
        out_ref[u, 0:32, :] = short[:, u * TILE : (u + 1) * TILE]
    lags = []
    per = TILE // GW
    lane = lax.broadcasted_iota(jnp.int32, (KL, TILE), 1) // GW
    for u in range(channels // TILE):
        grad = send_ref[0:KL, u * TILE : (u + 1) * TILE].astype(F32)
        stacked = jnp.concatenate(
            [jnp.where(lane == g, grad, 0.0).astype(BF) for g in range(per)], axis=0
        )
        skew_ref[...] = dot_nt(stacked, turned_ref[:, u * TILE : (u + 1) * TILE])
        for g in range(per):
            rolled = pltpu.roll(skew_ref[g * KL : (g + 1) * KL, :], 0, 1, stride=1, stride_axis=0)
            lags.append(jnp.sum(rolled, axis=0, keepdims=True))
    if groups < GW:
        lags.append(jnp.zeros((GW - groups, WIN), F32))
    sums = pltpu.roll(jnp.concatenate(lags, axis=0), WIN - (KL - 1), 1)
    long = sums[:, :KL].astype(BF)
    for u in range(channels // TILE):
        out_ref[u, 32:AUX, :] = long


def sum_body(copies, in_ref, out_ref):
    total = in_ref[0].astype(F32)
    for s in range(1, in_ref.shape[0]):
        total = total + in_ref[s].astype(F32)
    value = total.astype(BF)
    for s in range(copies):
        out_ref[s] = value


def merge_body(sums_ref, *refs):
    grads, out_ref = refs[:-1], refs[-1]
    halves = sums_ref.shape[0] // len(grads)
    for p, ref in enumerate(grads):
        out_ref[p, :KL, :] = ref[...]
        for u in range(halves):
            out_ref[p, KL:, u * TILE : (u + 1) * TILE] = sums_ref[p * halves + u]


def spread_body(slices, width, in_ref, grad_ref, short_ref, long_ref):
    planes = in_ref.shape[0]
    matrix = swap_matrix(width)
    grad_ref[...] = join_owned([in_ref[z, :KL] for z in range(planes)], width, matrix).astype(BF)
    short = join_owned([in_ref[z, KL : KL + 32] for z in range(planes)], width, matrix)
    for j in range(KS):
        short_ref[j, 0:3, :] = short[3 * j : 3 * j + 3]
    per = width // GW
    groups = slices * per
    stacked = jnp.concatenate(
        [in_ref[z, KL + 32 : KL + 32 + groups, :KL] for z in range(planes)], axis=0
    )
    mover = filter_rows(slices, planes, per)
    long_ref[...] = lax.dot_general(
        mover, stacked, (((0,), (0,)), ((), ())), preferred_element_type=F32
    )


def from_next(x, by):
    size = lax.axis_size("seq")
    return lax.ppermute(x, "seq", [(i, i - by) for i in range(by, size)])


def from_before(x, by):
    size = lax.axis_size("seq")
    return lax.ppermute(x, "seq", [(i, i + by) for i in range(size - by)])


def per_device(layer_inputs, out_grad, short_weights, long_filters, out_weights):
    planes = lax.axis_size("pipe")
    blocks = lax.axis_size("seq")
    depth = out_weights.shape[2]
    half = out_grad.shape[1]
    width = depth // planes
    slices = half // depth
    owned = slices * width
    groups = owned // GW
    tokens = out_grad.shape[0]
    dims = long_filters.shape[1]

    tp_index = lax.axis_index("tp").astype(jnp.int32).reshape(1)
    own_rows = layer_inputs[0]
    swapped = lax.ppermute(own_rows, "tp", [(0, 1), (1, 0)])
    packed = pl.pallas_call(
        functools.partial(pack_body, planes, slices, width),
        out_shape=shape((planes, tokens + depth + AUX, owned), BF),
        in_specs=[pl.BlockSpec(memory_space=pltpu.SMEM)]
        + [pl.BlockSpec(memory_space=pltpu.VMEM)] * 5,
        compiler_params=pltpu.CompilerParams(vmem_limit_bytes=VMEM_LIMIT),
        interpret=INTERPRET,
    )(
        tp_index,
        out_weights[0].reshape(slices, planes, width, depth),
        short_weights[0],
        long_filters[0],
        own_rows,
        swapped,
    )
    packed = lax.all_to_all(packed, "pipe", 0, 0, tiled=True)
    rows = packed[:, :tokens]
    before = from_before(rows, 1)
    before2 = from_before(rows[:, tokens - PAD :], 2)
    after = from_next(rows[:, :PAD], 1)

    def whole(x):
        return pl.BlockSpec(x.shape, lambda i: (0,) * len(x.shape))

    def plane(x, p, count, at=0):
        return pl.BlockSpec((None, count, x.shape[2]), lambda i, p=p, at=at: (p, at, 0))

    def own_block(p):
        return plane(packed, p, tokens)

    def aux_block(p):
        return plane(packed, p, AUX, (tokens + depth) // AUX)

    def recomputed(p):
        results = (
            shape((KL, owned), F32),
            shape((KL + EDGE, owned), F32),
            shape((KL + EDGE, owned), F32),
            shape((KL + EDGE, owned), F32),
            shape((groups * KL, WIN), BF),
            shape((WIN, owned), BF),
        )
        return call(
            functools.partial(recompute_body, groups),
            results,
            packed,
            before,
            before2,
            after,
            packed,
            grid=(1,),
            in_specs=[
                own_block(p),
                plane(before, p, tokens),
                plane(before2, p, PAD),
                plane(after, p, PAD),
                aux_block(p),
            ],
            out_specs=tuple(whole(r) for r in results),
            scratch_shapes=[
                pltpu.VMEM((2 * KL + 2 * PAD, owned), F32),
                pltpu.VMEM((groups * KL, WIN), BF),
            ],
        )

    def gathered(source, first, last):
        pieces = lax.all_gather(source[first : last + 1, tokens : tokens + depth], "seq", axis=0)
        return pieces.reshape(blocks, last + 1 - first, planes, width, owned)

    def copied(p):
        copies = jnp.broadcast_to(packed[p, tokens : tokens + depth][None], (blocks, depth, owned))
        pieces = lax.all_to_all(copies, "seq", 0, 0, tiled=True)
        return pieces.reshape(blocks, 1, planes, width, owned)

    starts = call(
        functools.partial(shuffle_body, planes, width),
        shape((planes, tokens, owned), BF),
        out_grad,
    )
    grad = lax.dynamic_index_in_dim(starts, lax.axis_index("pipe"), 0, keepdims=False)
    swap = [(0, 1), (1, 0)]
    other = lax.ppermute(grad, "tp", swap)

    saved = {planes - 1: recomputed(planes - 1)}
    first_weights, saved[planes - 1], source, grad, other = lax.optimization_barrier(
        (copied(planes - 1), saved[planes - 1], packed, grad, other)
    )
    weights = {planes - 1: (first_weights, 0)}
    last = planes - 2
    for size in (2, 3, planes):
        first = max(0, last - size + 1)
        if last >= first:
            group = gathered(source, first, last)
            weights.update({p: (group, p - first) for p in range(first, last + 1)})
        last = first - 1

    def filter_sums(p, operands, sums):
        halves = owned // TILE
        result = shape((planes * halves, AUX, TILE), BF)
        operands = [*operands[:5], packed, before, *operands[5:]]
        specs = [whole(x) for x in operands]
        specs[5:7] = [own_block(p), plane(before, p, tokens)]
        aliases = {}
        if sums is not None:
            aliases = {len(operands): 0}
            operands.append(sums)
            specs.append(pl.BlockSpec(memory_space=pl.ANY))
        return call(
            functools.partial(filters_body, groups),
            result,
            *operands,
            grid=(1,),
            in_specs=specs,
            out_specs=pl.BlockSpec((halves, AUX, TILE), lambda i, p=p: (p, 0, 0)),
            input_output_aliases=aliases,
            scratch_shapes=[
                pltpu.VMEM((KL + PAD, owned), F32),
                pltpu.VMEM((TILE // GW * KL, WIN), F32),
            ],
        )

    outs = [None] * planes
    sums = None
    late = None
    for p in range(planes - 1, -1, -1):
        group, at = weights[p]
        for q in range(p, max(p - 4, -1) if p == planes - 2 else p - 1, -1):
            if q not in saved:
                saved[q] = recomputed(q)
                if p == planes - 2:
                    group, saved[q] = lax.optimization_barrier((group, saved[q]))
        f0, f1, f2, mixed, back, turned = saved[p]
        if p + 1 < planes:
            other = lax.ppermute(grad, "tp", swap)
        partial = pl.pallas_call(
            project_body,
            out_shape=shape((planes, tokens, owned), BF),
            grid_spec=pltpu.PrefetchScalarGridSpec(
                num_scalar_prefetch=1,
                grid=(2,),
                in_specs=[
                    pl.BlockSpec((tokens, owned), lambda z, t: (0, 0)),
                    pl.BlockSpec((tokens, owned), lambda z, t: (0, 0)),
                    pl.BlockSpec(
                        (blocks, 1, planes // 2, width, owned), lambda z, t, at=at: (0, at, z, 0, 0)
                    ),
                ],
                out_specs=pl.BlockSpec((planes // 2, tokens, owned), lambda z, t: (z, 0, 0)),
            ),
            compiler_params=pltpu.CompilerParams(vmem_limit_bytes=VMEM_LIMIT),
            interpret=INTERPRET,
        )(tp_index, grad, other, group)
        parts = lax.all_to_all(partial, "pipe", 0, 0, tiled=True)
        send, dgate, early = call(
            gate_body,
            (
                shape((KL + PAD, owned), BF),
                shape((KL, owned), BF),
                shape((PAD, owned), BF),
            ),
            parts,
            f0,
        )
        near = from_next(send, 1)
        far = from_next(early, 2)
        if late is not None:
            send, late[0] = lax.optimization_barrier((send, late[0]))
            sums = filter_sums(p + 1, late, sums)
            near, sums = lax.optimization_barrier((near, sums))
        results = (shape((KL, owned), BF), shape((KL, owned), F32))
        operands = (send, dgate, near, far, f1, f2, mixed, back, packed, grad)
        new_grad, dkv = call(
            functools.partial(finish_body, groups),
            results,
            *operands,
            grid=(1,),
            in_specs=[aux_block(p) if x is packed else whole(x) for x in operands],
            out_specs=tuple(whole(r) for r in results),
            scratch_shapes=[pltpu.VMEM((KL + EDGE, owned), F32)] * 3,
        )
        late = [dgate, mixed, dkv, f1, f2, send, turned]
        outs[p] = new_grad
        grad = new_grad

    sums = filter_sums(0, late, sums)
    exchanged = lax.all_to_all(sums, "seq", 0, 0, tiled=True)
    summed = call(
        functools.partial(sum_body, blocks), shape((blocks, AUX, TILE), BF), exchanged
    )
    summed = lax.all_to_all(summed, "seq", 0, 0, tiled=True)
    merged = call(merge_body, shape((planes, tokens + AUX, owned), BF), summed, *outs)
    results = lax.all_to_all(merged, "pipe", 0, 0, tiled=True)
    input_grad, short_result, long_result = call(
        functools.partial(spread_body, slices, width),
        (shape((tokens, half), BF), shape((KS, 8, half), F32), shape((dims, KL), F32)),
        results,
    )
    return input_grad[None], short_result[None, :, :3], long_result[None]


def solution(mesh):
    in_specs = (
        P("pipe", ("seq", "tp"), None),
        P("seq", "tp"),
        P("pipe", None, None, "tp"),
        P("pipe", "tp", None),
        P("pipe", "tp", "seq"),
    )
    out_specs = (P("pipe", "seq", "tp"), P("pipe", None, None, "tp"), P("pipe", "tp", None))
    return jax.shard_map(
        per_device, mesh=mesh, in_specs=in_specs, out_specs=out_specs, check_vma=False
    )
```

```python
import functools

import jax
import jax.numpy as jnp
from jax import lax
from jax.experimental import pallas as pl
from jax.experimental.pallas import tpu as pltpu
from jax.sharding import PartitionSpec as P

KL = 128
KS = 7
TILE = 128
GW = 16
AUX = 48
EDGE = 8
REACH = KL + EDGE
PAD = 16
WIN = 2 * KL
BF = jnp.bfloat16
F32 = jnp.float32
VMEM_LIMIT = 24 * 1024 * 1024
INTERPRET = False


def call(body, out_shape, *args, **kwargs):
    return pl.pallas_call(
        body,
        out_shape=out_shape,
        compiler_params=pltpu.CompilerParams(vmem_limit_bytes=VMEM_LIMIT),
        interpret=INTERPRET,
        **kwargs,
    )(*args)


def shape(dims, dtype):
    return jax.ShapeDtypeStruct(dims, dtype)


def dot(a, b):
    return jnp.dot(a, b, preferred_element_type=F32)


def dot_nt(a, b):
    return lax.dot_general(a, b, (((1,), (1,)), ((), ())), preferred_element_type=F32)


def swap_matrix(width):
    size = TILE // width
    n = size * TILE
    row = lax.broadcasted_iota(jnp.int32, (n, n), 0)
    col = lax.broadcasted_iota(jnp.int32, (n, n), 1)
    a, b, j = row // TILE, (row // width) % size, row % width
    return (col == b * TILE + a * width + j).astype(F32).astype(BF)


def split_owned(x, planes, width, matrix):
    step = planes * width
    slices = x.shape[1] // step
    size = TILE // width
    pieces = [[None] * (slices // size) for _ in range(planes)]
    for a in range(slices // size):
        for b in range(planes // size):
            tiles = [
                x[:, (a * size + i) * step + b * TILE : (a * size + i) * step + (b + 1) * TILE]
                for i in range(size)
            ]
            moved = dot(jnp.concatenate(tiles, axis=1), matrix).astype(BF)
            for i in range(size):
                pieces[b * size + i][a] = moved[:, i * TILE : (i + 1) * TILE]
    return [jnp.concatenate(p, axis=1) for p in pieces]


def join_owned(parts, width, matrix):
    planes = len(parts)
    size = TILE // width
    slices = parts[0].shape[1] // width
    out = [[None] * (planes // size) for _ in range(slices)]
    for a in range(slices // size):
        for b in range(planes // size):
            tiles = [parts[b * size + i][:, a * TILE : (a + 1) * TILE] for i in range(size)]
            moved = dot(jnp.concatenate(tiles, axis=1), matrix)
            for i in range(size):
                out[a * size + i][b] = moved[:, i * TILE : (i + 1) * TILE]
    return jnp.concatenate([jnp.concatenate(o, axis=1) for o in out], axis=1)


def filter_rows(slices, planes, per):
    n = slices * planes * per
    row = lax.broadcasted_iota(jnp.int32, (n, n), 0)
    col = lax.broadcasted_iota(jnp.int32, (n, n), 1)
    z, k, g = row // (slices * per), (row // per) % slices, row % per
    return (col == k * planes * per + z * per + g).astype(F32).astype(BF)


def pack_body(planes, slices, width, tp_ref, w_ref, sw_ref, lf_ref, x_ref, other_ref, out_ref):
    owned = slices * width
    depth = planes * width
    half = slices * depth
    count = x_ref.shape[0]
    matrix = swap_matrix(width)
    tp = tp_ref[0]
    start = pl.multiple_of(tp * half, TILE)
    for source, place in ((x_ref, tp), (other_ref, 1 - tp)):
        pieces = split_owned(source[:, pl.ds(start, half)], planes, width, matrix)
        at = pl.multiple_of(place * count, PAD)
        for z in range(planes):
            out_ref[z, pl.ds(at, count), :] = pieces[z]
    for z in range(planes):
        block = w_ref[:, z].reshape(owned, depth)
        turned = block.astype(F32).T.astype(BF)
        low = KL + z * width
        out_ref[:, low : low + width, :] = turned.reshape(planes, width, owned)
    base = KL + depth
    taps = [sw_ref[j].astype(F32) for j in range(KS)]
    taps.append(jnp.zeros((32 - 3 * KS, half), F32))
    taps = split_owned(jnp.concatenate(taps, axis=0).astype(BF), planes, width, matrix)
    per = width // GW
    filters = dot(filter_rows(slices, planes, per), lf_ref[...]).astype(BF)
    groups = slices * per
    for z in range(planes):
        out_ref[z, base : base + 32, :] = taps[z]
        out_ref[z, base + 32 : base + AUX, :] = jnp.zeros((GW, owned), BF)
        out_ref[z, base + 32 : base + 32 + groups, :KL] = filters[z * groups : (z + 1) * groups]


def shuffle_body(planes, width, x_ref, out_ref):
    pieces = split_owned(x_ref[...], planes, width, swap_matrix(width))
    for z in range(planes):
        out_ref[z] = pieces[z]


def grouped(toeplitz, rows_per, source, groups):
    channels = source.shape[1]
    tiles = []
    for u in range(channels // TILE):
        per = TILE // GW
        full = dot(toeplitz[u * per * rows_per : (u + 1) * per * rows_per], source[:, u * TILE : (u + 1) * TILE])
        lane = lax.broadcasted_iota(jnp.int32, (rows_per, TILE), 1) // GW
        merged = full[:rows_per]
        for g in range(1, per):
            merged = jnp.where(lane == g, full[g * rows_per : (g + 1) * rows_per], merged)
        tiles.append(merged)
    return jnp.concatenate(tiles, axis=1)


def edge_rows(ref, groups):
    return jnp.concatenate(
        [ref[g * KL + KL - PAD : (g + 1) * KL, :] for g in range(groups)], axis=0
    )


def recompute_body(
    groups, own_ref, prev_ref, prev2_ref, next_ref, aux_ref, features_ref, back_ref, rows_ref, band_ref,
):
    rows_ref[0:PAD, :] = prev2_ref[...].astype(F32)
    rows_ref[PAD : PAD + KL, :] = prev_ref[...].astype(F32)
    rows_ref[PAD + KL : PAD + 2 * KL, :] = own_ref[...].astype(F32)
    rows_ref[PAD + 2 * KL :, :] = next_ref[...].astype(F32)
    taps = aux_ref[0:32, :].astype(F32)

    def feature(f, first, count):
        start = PAD + KL + first
        total = taps[f : f + 1] * rows_ref[start : start + count, :]
        for j in range(1, KS):
            total = total + taps[3 * j + f : 3 * j + f + 1] * rows_ref[start - j : start - j + count, :]
        return total

    features_ref[0:REACH, :] = feature(0, 0, REACH)
    key_tail = feature(1, 0, REACH)
    value_tail = feature(2, 0, REACH)
    features_ref[REACH : 2 * REACH, :] = key_tail
    features_ref[2 * REACH : 3 * REACH, :] = value_tail
    kv = jnp.concatenate([feature(1, -KL, KL) * feature(2, -KL, KL), key_tail * value_tail], axis=0)
    window = kv[:WIN].astype(BF)
    late = kv[EDGE : EDGE + WIN].astype(BF)

    filters = aux_ref[32 : 32 + groups, :KL]
    tap = lax.broadcasted_iota(jnp.int32, (KL, WIN), 0)
    lane = lax.broadcasted_iota(jnp.int32, (KL, WIN), 1)
    ahead = dot(filters, (lane == KL - tap).astype(F32).astype(BF))
    behind = dot(filters, (lane == tap).astype(F32).astype(BF))
    for g in range(groups):
        wide = jnp.broadcast_to(ahead[g : g + 1], (KL, WIN))
        band_ref[g * KL : (g + 1) * KL, :] = pltpu.roll(wide, 0, 1, stride=1, stride_axis=0).astype(BF)
        wide = jnp.broadcast_to(behind[g : g + 1], (KL, WIN))
        back_ref[g * KL : (g + 1) * KL, :] = pltpu.roll(wide, 0, 1, stride=1, stride_axis=0).astype(BF)
    features_ref[3 * REACH : 3 * REACH + KL, :] = grouped(band_ref, KL, window, groups)
    features_ref[3 * REACH + KL :, :] = grouped(edge_rows(band_ref, groups), PAD, late, groups)[PAD - EDGE :]
    source = lax.broadcasted_iota(jnp.int32, (WIN, WIN), 0)
    target = lax.broadcasted_iota(jnp.int32, (WIN, WIN), 1)
    mirror = (source + target == WIN - 1).astype(F32).astype(BF)
    back_ref[groups * KL :, :] = dot(mirror, window).astype(BF)


def project_body(tp_ref, own_ref, other_ref, w_ref, out_ref):
    first = tp_ref[0] == 0
    own, other = own_ref[...], other_ref[...]
    rows = jnp.concatenate([jnp.where(first, own, other), jnp.where(first, other, own)], axis=1)
    slices, _, count, width, owned = w_ref.shape
    for z in range(count):
        out_ref[z] = dot(rows, w_ref[:, 0, z].reshape(slices * width, owned)).astype(BF)


def gate_body(parts_ref, features_ref, send_ref, dgate_ref, early_ref):
    total = parts_ref[0].astype(F32)
    for z in range(1, parts_ref.shape[0]):
        total = total + parts_ref[z].astype(F32)
    dgate = total.astype(BF)
    dmixed = (dgate.astype(F32) * features_ref[0:KL, :]).astype(BF)
    send_ref[0:KL, :] = dmixed
    send_ref[KL:, :] = dgate[:PAD]
    dgate_ref[...] = dgate
    early_ref[...] = dmixed[:PAD]


def finish_body(
    groups, send_ref, dgate_ref, near_ref, far_ref, features_ref, back_ref, aux_ref, grad_ref,
    out_ref, trail_ref, d0_ref, d1_ref, d2_ref,
):
    rows = jnp.concatenate(
        [send_ref[0:KL, :], near_ref[0:KL, :], far_ref[...]], axis=0
    )
    window = rows[:WIN]
    late = rows.astype(F32)[EDGE : EDGE + WIN].astype(BF)
    main = grouped(back_ref, KL, window, groups)
    tail = grouped(edge_rows(back_ref, groups), PAD, late, groups)[PAD - EDGE :]
    key, value, mixed = REACH, 2 * REACH, 3 * REACH
    d0_ref[0:KL, :] = dgate_ref[...].astype(F32) * features_ref[mixed : mixed + KL, :]
    d0_ref[KL:, :] = near_ref[KL:, :].astype(F32)[:EDGE] * features_ref[mixed + KL :, :]
    d1_ref[0:KL, :] = main * features_ref[value : value + KL, :]
    d1_ref[KL:, :] = tail * features_ref[value + KL : mixed, :]
    d2_ref[0:KL, :] = main * features_ref[key : key + KL, :]
    d2_ref[KL:, :] = tail * features_ref[key + KL : value, :]
    taps = aux_ref[0:32, :].astype(F32)
    total = grad_ref[...].astype(F32)
    for f, ref in enumerate((d0_ref, d1_ref, d2_ref)):
        trail_ref[f * KL : (f + 1) * KL, :] = ref[0:KL, :]
        for j in range(KS):
            total = total + taps[3 * j + f : 3 * j + f + 1] * ref[j : j + KL, :]
    out_ref[...] = total.astype(BF)


def filters_body(
    groups, trail_ref, send_ref, back_ref, own_ref, prev_ref, *refs,
):
    out_ref, rows_ref, skew_ref = refs[-3:]
    channels = own_ref.shape[1]
    rows_ref[0:PAD, :] = prev_ref[...].astype(F32)
    rows_ref[PAD:, :] = own_ref[...].astype(F32)
    sums = []
    for j in range(KS):
        source = rows_ref[PAD - j : PAD - j + KL, :]
        for f in range(3):
            grads = trail_ref[f * KL : (f + 1) * KL, :]
            sums.append(jnp.sum(grads * source, axis=0, keepdims=True))
    sums.append(jnp.zeros((32 - 3 * KS, channels), F32))
    short = jnp.concatenate(sums, axis=0).astype(BF)
    for u in range(channels // TILE):
        out_ref[u, 0:32, :] = short[:, u * TILE : (u + 1) * TILE]
    lags = []
    per = TILE // GW
    lane = lax.broadcasted_iota(jnp.int32, (KL, TILE), 1) // GW
    for u in range(channels // TILE):
        grad = send_ref[0:KL, u * TILE : (u + 1) * TILE].astype(F32)
        stacked = jnp.concatenate(
            [jnp.where(lane == g, grad, 0.0).astype(BF) for g in range(per)], axis=0
        )
        skew_ref[...] = dot_nt(stacked, back_ref[groups * KL :, u * TILE : (u + 1) * TILE])
        for g in range(per):
            rolled = pltpu.roll(skew_ref[g * KL : (g + 1) * KL, :], 0, 1, stride=1, stride_axis=0)
            lags.append(jnp.sum(rolled, axis=0, keepdims=True))
    if groups < GW:
        lags.append(jnp.zeros((GW - groups, WIN), F32))
    sums = pltpu.roll(jnp.concatenate(lags, axis=0), WIN - (KL - 1), 1)
    long = sums[:, :KL].astype(BF)
    for u in range(channels // TILE):
        out_ref[u, 32:AUX, :] = long


def sum_body(copies, in_ref, out_ref):
    total = in_ref[0].astype(F32)
    for s in range(1, in_ref.shape[0]):
        total = total + in_ref[s].astype(F32)
    value = total.astype(BF)
    for s in range(copies):
        out_ref[s] = value


def merge_body(sums_ref, *refs):
    grads, out_ref = refs[:-1], refs[-1]
    halves = sums_ref.shape[0] // len(grads)
    for p, ref in enumerate(grads):
        out_ref[p, :KL, :] = ref[...]
        for u in range(halves):
            out_ref[p, KL:, u * TILE : (u + 1) * TILE] = sums_ref[p * halves + u]


def spread_body(slices, width, in_ref, grad_ref, short_ref, long_ref):
    planes = in_ref.shape[0]
    matrix = swap_matrix(width)
    grad_ref[...] = join_owned([in_ref[z, :KL] for z in range(planes)], width, matrix).astype(BF)
    short = join_owned([in_ref[z, KL : KL + 32] for z in range(planes)], width, matrix)
    for j in range(KS):
        short_ref[j, 0:3, :] = short[3 * j : 3 * j + 3]
    per = width // GW
    groups = slices * per
    stacked = jnp.concatenate(
        [in_ref[z, KL + 32 : KL + 32 + groups, :KL] for z in range(planes)], axis=0
    )
    mover = filter_rows(slices, planes, per)
    long_ref[...] = lax.dot_general(
        mover, stacked, (((0,), (0,)), ((), ())), preferred_element_type=F32
    )


def from_next(x, by):
    size = lax.axis_size("seq")
    return lax.ppermute(x, "seq", [(i, i - by) for i in range(by, size)])


def from_before(x, by):
    size = lax.axis_size("seq")
    return lax.ppermute(x, "seq", [(i, i + by) for i in range(size - by)])


def per_device(layer_inputs, out_grad, short_weights, long_filters, out_weights):
    planes = lax.axis_size("pipe")
    blocks = lax.axis_size("seq")
    depth = out_weights.shape[2]
    half = out_grad.shape[1]
    width = depth // planes
    slices = half // depth
    owned = slices * width
    groups = owned // GW
    tokens = out_grad.shape[0]
    dims = long_filters.shape[1]

    tp_index = lax.axis_index("tp").astype(jnp.int32).reshape(1)
    own_rows = layer_inputs[0]
    swapped = lax.ppermute(own_rows, "tp", [(0, 1), (1, 0)])
    packed = pl.pallas_call(
        functools.partial(pack_body, planes, slices, width),
        out_shape=shape((planes, tokens + depth + AUX, owned), BF),
        in_specs=[pl.BlockSpec(memory_space=pltpu.SMEM)]
        + [pl.BlockSpec(memory_space=pltpu.VMEM)] * 5,
        compiler_params=pltpu.CompilerParams(vmem_limit_bytes=VMEM_LIMIT),
        interpret=INTERPRET,
    )(
        tp_index,
        out_weights[0].reshape(slices, planes, width, depth),
        short_weights[0],
        long_filters[0],
        own_rows,
        swapped,
    )
    packed = lax.all_to_all(packed, "pipe", 0, 0, tiled=True)
    top = planes - 1

    def surroundings(rows):
        return (
            from_before(rows, 1),
            from_before(rows[:, tokens - PAD :], 2),
            from_next(rows[:, :PAD], 1),
        )

    def whole(x):
        return pl.BlockSpec(x.shape, lambda i: (0,) * len(x.shape))

    def plane(x, p, count, at=0):
        return pl.BlockSpec((None, count, x.shape[2]), lambda i, p=p, at=at: (p, at, 0))

    def own_block(p):
        return plane(packed, p, tokens)

    def aux_block(p):
        return plane(packed, p, AUX, (tokens + depth) // AUX)

    def recomputed(p, around, at):
        results = (shape((4 * REACH, owned), F32), shape((groups * KL + WIN, owned), BF))
        before, before2, after = around
        return call(
            functools.partial(recompute_body, groups),
            results,
            packed,
            before,
            before2,
            after,
            packed,
            grid=(1,),
            in_specs=[
                own_block(p),
                plane(before, at, tokens),
                plane(before2, at, PAD),
                plane(after, at, PAD),
                aux_block(p),
            ],
            out_specs=tuple(whole(r) for r in results),
            scratch_shapes=[
                pltpu.VMEM((2 * KL + 2 * PAD, owned), F32),
                pltpu.VMEM((groups * KL, WIN), BF),
            ],
        )

    def gathered(source, first, last):
        pieces = lax.all_gather(source[first : last + 1, tokens : tokens + depth], "seq", axis=0)
        return pieces.reshape(blocks, last + 1 - first, planes, width, owned)

    def copied(p):
        copies = jnp.broadcast_to(packed[p, tokens : tokens + depth][None], (blocks, depth, owned))
        pieces = lax.all_to_all(copies, "seq", 0, 0, tiled=True)
        return pieces.reshape(blocks, 1, planes, width, owned)

    starts = call(
        functools.partial(shuffle_body, planes, width),
        shape((planes, tokens, owned), BF),
        out_grad,
    )
    grad = lax.dynamic_index_in_dim(starts, lax.axis_index("pipe"), 0, keepdims=False)
    swap = [(0, 1), (1, 0)]
    other = lax.ppermute(grad, "tp", swap)

    around = {top: (surroundings(packed[top:, :tokens]), 0)}
    saved = {top: recomputed(top, *around[top])}
    first_weights, saved[top], source, grad, other = lax.optimization_barrier(
        (copied(top), saved[top], packed, grad, other)
    )
    others = surroundings(source[:top, :tokens])
    around.update({p: (others, p) for p in range(top)})
    weights = {top: (first_weights, 0)}
    last = planes - 2
    for size in (2, 3, planes):
        first = max(0, last - size + 1)
        if last >= first:
            group = gathered(source, first, last)
            weights.update({p: (group, p - first) for p in range(first, last + 1)})
        last = first - 1

    def filter_sums(p, operands, sums):
        halves = owned // TILE
        result = shape((planes * halves, AUX, TILE), BF)
        (before, _, _), at = around[p]
        specs = [whole(x) for x in operands]
        specs += [own_block(p), plane(before, at, PAD, tokens // PAD - 1)]
        operands = [*operands, packed, before]
        aliases = {}
        if sums is not None:
            aliases = {len(operands): 0}
            operands.append(sums)
            specs.append(pl.BlockSpec(memory_space=pl.ANY))
        return call(
            functools.partial(filters_body, groups),
            result,
            *operands,
            grid=(1,),
            in_specs=specs,
            out_specs=pl.BlockSpec((halves, AUX, TILE), lambda i, p=p: (p, 0, 0)),
            input_output_aliases=aliases,
            scratch_shapes=[
                pltpu.VMEM((KL + PAD, owned), F32),
                pltpu.VMEM((TILE // GW * KL, WIN), F32),
            ],
        )

    outs = [None] * planes
    sums = None
    late = None
    for p in range(planes - 1, -1, -1):
        group, at = weights[p]
        if p == top - 1:
            for q in range(top):
                saved[q] = recomputed(q, *around[q])
            group, saved = lax.optimization_barrier((group, saved))
        features, back = saved[p]
        if p + 1 < planes:
            other = lax.ppermute(grad, "tp", swap)
        partial = pl.pallas_call(
            project_body,
            out_shape=shape((planes, tokens, owned), BF),
            grid_spec=pltpu.PrefetchScalarGridSpec(
                num_scalar_prefetch=1,
                grid=(2,),
                in_specs=[
                    pl.BlockSpec((tokens, owned), lambda z, t: (0, 0)),
                    pl.BlockSpec((tokens, owned), lambda z, t: (0, 0)),
                    pl.BlockSpec(
                        (blocks, 1, planes // 2, width, owned), lambda z, t, at=at: (0, at, z, 0, 0)
                    ),
                ],
                out_specs=pl.BlockSpec((planes // 2, tokens, owned), lambda z, t: (z, 0, 0)),
            ),
            compiler_params=pltpu.CompilerParams(vmem_limit_bytes=VMEM_LIMIT),
            interpret=INTERPRET,
        )(tp_index, grad, other, group)
        parts = lax.all_to_all(partial, "pipe", 0, 0, tiled=True)
        send, dgate, early = call(
            gate_body,
            (
                shape((KL + PAD, owned), BF),
                shape((KL, owned), BF),
                shape((PAD, owned), BF),
            ),
            parts,
            features,
        )
        near = from_next(send, 1)
        far = from_next(early, 2)
        if late is not None:
            send, late[0] = lax.optimization_barrier((send, late[0]))
            sums = filter_sums(p + 1, late, sums)
            near, sums = lax.optimization_barrier((near, sums))
        results = (shape((KL, owned), BF), shape((3 * KL, owned), F32))
        operands = (send, dgate, near, far, features, back, packed, grad)
        new_grad, trail = call(
            functools.partial(finish_body, groups),
            results,
            *operands,
            grid=(1,),
            in_specs=[aux_block(p) if x is packed else whole(x) for x in operands],
            out_specs=tuple(whole(r) for r in results),
            scratch_shapes=[pltpu.VMEM((REACH, owned), F32)] * 3,
        )
        late = [trail, send, back]
        outs[p] = new_grad
        grad = new_grad

    sums = filter_sums(0, late, sums)
    exchanged = lax.all_to_all(sums, "seq", 0, 0, tiled=True)
    summed = call(
        functools.partial(sum_body, blocks), shape((blocks, AUX, TILE), BF), exchanged
    )
    summed = lax.all_to_all(summed, "seq", 0, 0, tiled=True)
    merged = call(merge_body, shape((planes, tokens + AUX, owned), BF), summed, *outs)
    results = lax.all_to_all(merged, "pipe", 0, 0, tiled=True)
    input_grad, short_result, long_result = call(
        functools.partial(spread_body, slices, width),
        (shape((tokens, half), BF), shape((KS, 8, half), F32), shape((dims, KL), F32)),
        results,
    )
    return input_grad[None], short_result[None, :, :3], long_result[None]


def solution(mesh):
    in_specs = (
        P("pipe", ("seq", "tp"), None),
        P("seq", "tp"),
        P("pipe", None, None, "tp"),
        P("pipe", "tp", None),
        P("pipe", "tp", "seq"),
    )
    out_specs = (P("pipe", "seq", "tp"), P("pipe", None, None, "tp"), P("pipe", "tp", None))
    return jax.shard_map(
        per_device, mesh=mesh, in_specs=in_specs, out_specs=out_specs, check_vma=False
    )
```

```python
import functools

import jax
import jax.numpy as jnp
from jax import lax
from jax.experimental import pallas as pl
from jax.experimental.pallas import tpu as pltpu
from jax.sharding import PartitionSpec as P

KL = 128
KS = 7
TILE = 128
GW = 16
AUX = 48
EDGE = 8
REACH = KL + EDGE
PAD = 16
WIN = 2 * KL
BF = jnp.bfloat16
F32 = jnp.float32
VMEM_LIMIT = 24 * 1024 * 1024
INTERPRET = False


def call(body, out_shape, *args, **kwargs):
    return pl.pallas_call(
        body,
        out_shape=out_shape,
        compiler_params=pltpu.CompilerParams(vmem_limit_bytes=VMEM_LIMIT),
        interpret=INTERPRET,
        **kwargs,
    )(*args)


def shape(dims, dtype):
    return jax.ShapeDtypeStruct(dims, dtype)


def dot(a, b):
    return jnp.dot(a, b, preferred_element_type=F32)


def dot_nt(a, b):
    return lax.dot_general(a, b, (((1,), (1,)), ((), ())), preferred_element_type=F32)


def swap_matrix(width):
    size = TILE // width
    n = size * TILE
    row = lax.broadcasted_iota(jnp.int32, (n, n), 0)
    col = lax.broadcasted_iota(jnp.int32, (n, n), 1)
    a, b, j = row // TILE, (row // width) % size, row % width
    return (col == b * TILE + a * width + j).astype(F32).astype(BF)


def split_owned(x, planes, width, matrix):
    step = planes * width
    slices = x.shape[1] // step
    size = TILE // width
    pieces = [[None] * (slices // size) for _ in range(planes)]
    for a in range(slices // size):
        for b in range(planes // size):
            tiles = [
                x[:, (a * size + i) * step + b * TILE : (a * size + i) * step + (b + 1) * TILE]
                for i in range(size)
            ]
            moved = dot(jnp.concatenate(tiles, axis=1), matrix).astype(BF)
            for i in range(size):
                pieces[b * size + i][a] = moved[:, i * TILE : (i + 1) * TILE]
    return [jnp.concatenate(p, axis=1) for p in pieces]


def join_owned(parts, width, matrix):
    planes = len(parts)
    size = TILE // width
    slices = parts[0].shape[1] // width
    out = [[None] * (planes // size) for _ in range(slices)]
    for a in range(slices // size):
        for b in range(planes // size):
            tiles = [parts[b * size + i][:, a * TILE : (a + 1) * TILE] for i in range(size)]
            moved = dot(jnp.concatenate(tiles, axis=1), matrix)
            for i in range(size):
                out[a * size + i][b] = moved[:, i * TILE : (i + 1) * TILE]
    return jnp.concatenate([jnp.concatenate(o, axis=1) for o in out], axis=1)


def filter_rows(slices, planes, per):
    n = slices * planes * per
    row = lax.broadcasted_iota(jnp.int32, (n, n), 0)
    col = lax.broadcasted_iota(jnp.int32, (n, n), 1)
    z, k, g = row // (slices * per), (row // per) % slices, row % per
    return (col == k * planes * per + z * per + g).astype(F32).astype(BF)


def pack_body(planes, slices, width, tp_ref, w_ref, sw_ref, lf_ref, x_ref, other_ref, out_ref):
    owned = slices * width
    depth = planes * width
    half = slices * depth
    count = x_ref.shape[0]
    matrix = swap_matrix(width)
    tp = tp_ref[0]
    start = pl.multiple_of(tp * half, TILE)
    for source, place in ((x_ref, tp), (other_ref, 1 - tp)):
        pieces = split_owned(source[:, pl.ds(start, half)], planes, width, matrix)
        at = pl.multiple_of(place * count, PAD)
        for z in range(planes):
            out_ref[z, pl.ds(at, count), :] = pieces[z]
    for z in range(planes):
        block = w_ref[:, z].reshape(owned, depth)
        turned = block.astype(F32).T.astype(BF)
        low = KL + z * width
        out_ref[:, low : low + width, :] = turned.reshape(planes, width, owned)
    base = KL + depth
    taps = [sw_ref[j].astype(F32) for j in range(KS)]
    taps.append(jnp.zeros((32 - 3 * KS, half), F32))
    taps = split_owned(jnp.concatenate(taps, axis=0).astype(BF), planes, width, matrix)
    per = width // GW
    filters = dot(filter_rows(slices, planes, per), lf_ref[...]).astype(BF)
    groups = slices * per
    for z in range(planes):
        out_ref[z, base : base + 32, :] = taps[z]
        out_ref[z, base + 32 : base + AUX, :] = jnp.zeros((GW, owned), BF)
        out_ref[z, base + 32 : base + 32 + groups, :KL] = filters[z * groups : (z + 1) * groups]


def shuffle_body(planes, width, x_ref, out_ref):
    pieces = split_owned(x_ref[...], planes, width, swap_matrix(width))
    for z in range(planes):
        out_ref[z] = pieces[z]


def grouped(toeplitz, rows_per, source, groups):
    channels = source.shape[1]
    tiles = []
    for u in range(channels // TILE):
        per = TILE // GW
        full = dot(toeplitz[u * per * rows_per : (u + 1) * per * rows_per], source[:, u * TILE : (u + 1) * TILE])
        lane = lax.broadcasted_iota(jnp.int32, (rows_per, TILE), 1) // GW
        merged = full[:rows_per]
        for g in range(1, per):
            merged = jnp.where(lane == g, full[g * rows_per : (g + 1) * rows_per], merged)
        tiles.append(merged)
    return jnp.concatenate(tiles, axis=1)


def edge_rows(ref, groups):
    return jnp.concatenate(
        [ref[g * KL + KL - PAD : (g + 1) * KL, :] for g in range(groups)], axis=0
    )


def recompute_body(
    groups, own_ref, prev_ref, prev2_ref, next_ref, aux_ref, features_ref, back_ref, rows_ref, band_ref,
):
    rows_ref[0:PAD, :] = prev2_ref[...].astype(F32)
    rows_ref[PAD : PAD + KL, :] = prev_ref[...].astype(F32)
    rows_ref[PAD + KL : PAD + 2 * KL, :] = own_ref[...].astype(F32)
    rows_ref[PAD + 2 * KL :, :] = next_ref[...].astype(F32)
    taps = aux_ref[0:32, :].astype(F32)

    def feature(f, first, count):
        start = PAD + KL + first
        total = taps[f : f + 1] * rows_ref[start : start + count, :]
        for j in range(1, KS):
            total = total + taps[3 * j + f : 3 * j + f + 1] * rows_ref[start - j : start - j + count, :]
        return total

    features_ref[0:REACH, :] = feature(0, 0, REACH)
    key_tail = feature(1, 0, REACH)
    value_tail = feature(2, 0, REACH)
    features_ref[REACH : 2 * REACH, :] = key_tail
    features_ref[2 * REACH : 3 * REACH, :] = value_tail
    kv = jnp.concatenate([feature(1, -KL, KL) * feature(2, -KL, KL), key_tail * value_tail], axis=0)
    window = kv[:WIN].astype(BF)
    late = kv[EDGE : EDGE + WIN].astype(BF)

    filters = aux_ref[32 : 32 + groups, :KL]
    tap = lax.broadcasted_iota(jnp.int32, (KL, WIN), 0)
    lane = lax.broadcasted_iota(jnp.int32, (KL, WIN), 1)
    ahead = dot(filters, (lane == KL - tap).astype(F32).astype(BF))
    behind = dot(filters, (lane == tap).astype(F32).astype(BF))
    for g in range(groups):
        wide = jnp.broadcast_to(ahead[g : g + 1], (KL, WIN))
        band_ref[g * KL : (g + 1) * KL, :] = pltpu.roll(wide, 0, 1, stride=1, stride_axis=0).astype(BF)
        wide = jnp.broadcast_to(behind[g : g + 1], (KL, WIN))
        back_ref[g * KL : (g + 1) * KL, :] = pltpu.roll(wide, 0, 1, stride=1, stride_axis=0).astype(BF)
    features_ref[3 * REACH : 3 * REACH + KL, :] = grouped(band_ref, KL, window, groups)
    features_ref[3 * REACH + KL :, :] = grouped(edge_rows(band_ref, groups), PAD, late, groups)[PAD - EDGE :]
    source = lax.broadcasted_iota(jnp.int32, (WIN, WIN), 0)
    target = lax.broadcasted_iota(jnp.int32, (WIN, WIN), 1)
    mirror = (source + target == WIN - 1).astype(F32).astype(BF)
    back_ref[groups * KL :, :] = dot(mirror, window).astype(BF)


def project_body(tp_ref, own_ref, other_ref, w_ref, out_ref):
    first = tp_ref[0] == 0
    own, other = own_ref[...], other_ref[...]
    rows = jnp.concatenate([jnp.where(first, own, other), jnp.where(first, other, own)], axis=1)
    slices, _, count, width, owned = w_ref.shape
    for z in range(count):
        out_ref[z] = dot(rows, w_ref[:, 0, z].reshape(slices * width, owned)).astype(BF)


def gate_body(parts_ref, features_ref, send_ref, dgate_ref, early_ref):
    total = parts_ref[0].astype(F32)
    for z in range(1, parts_ref.shape[0]):
        total = total + parts_ref[z].astype(F32)
    dgate = total.astype(BF)
    dmixed = (dgate.astype(F32) * features_ref[0:KL, :]).astype(BF)
    send_ref[0:KL, :] = dmixed
    send_ref[KL:, :] = dgate[:PAD]
    dgate_ref[...] = dgate
    early_ref[...] = dmixed[:PAD]


def finish_body(
    groups, send_ref, dgate_ref, near_ref, far_ref, features_ref, back_ref, aux_ref, grad_ref,
    out_ref, trail_ref, d0_ref, d1_ref, d2_ref,
):
    rows = jnp.concatenate(
        [send_ref[0:KL, :], near_ref[0:KL, :], far_ref[...]], axis=0
    )
    window = rows[:WIN]
    late = rows.astype(F32)[EDGE : EDGE + WIN].astype(BF)
    main = grouped(back_ref, KL, window, groups)
    tail = grouped(edge_rows(back_ref, groups), PAD, late, groups)[PAD - EDGE :]
    key, value, mixed = REACH, 2 * REACH, 3 * REACH
    d0_ref[0:KL, :] = dgate_ref[...].astype(F32) * features_ref[mixed : mixed + KL, :]
    d0_ref[KL:, :] = near_ref[KL:, :].astype(F32)[:EDGE] * features_ref[mixed + KL :, :]
    d1_ref[0:KL, :] = main * features_ref[value : value + KL, :]
    d1_ref[KL:, :] = tail * features_ref[value + KL : mixed, :]
    d2_ref[0:KL, :] = main * features_ref[key : key + KL, :]
    d2_ref[KL:, :] = tail * features_ref[key + KL : value, :]
    taps = aux_ref[0:32, :].astype(F32)
    total = grad_ref[...].astype(F32)
    for f, ref in enumerate((d0_ref, d1_ref, d2_ref)):
        trail_ref[f * KL : (f + 1) * KL, :] = ref[0:KL, :]
        for j in range(KS):
            total = total + taps[3 * j + f : 3 * j + f + 1] * ref[j : j + KL, :]
    out_ref[...] = total.astype(BF)


def filters_body(
    groups, trail_ref, send_ref, back_ref, own_ref, prev_ref, *refs,
):
    out_ref, rows_ref, skew_ref = refs[-3:]
    channels = own_ref.shape[1]
    rows_ref[0:PAD, :] = prev_ref[...].astype(F32)
    rows_ref[PAD:, :] = own_ref[...].astype(F32)
    sums = []
    for j in range(KS):
        source = rows_ref[PAD - j : PAD - j + KL, :]
        for f in range(3):
            grads = trail_ref[f * KL : (f + 1) * KL, :]
            sums.append(jnp.sum(grads * source, axis=0, keepdims=True))
    sums.append(jnp.zeros((32 - 3 * KS, channels), F32))
    short = jnp.concatenate(sums, axis=0).astype(BF)
    for u in range(channels // TILE):
        out_ref[u, 0:32, :] = short[:, u * TILE : (u + 1) * TILE]
    lags = []
    per = TILE // GW
    lane = lax.broadcasted_iota(jnp.int32, (KL, TILE), 1) // GW
    for u in range(channels // TILE):
        grad = send_ref[0:KL, u * TILE : (u + 1) * TILE].astype(F32)
        stacked = jnp.concatenate(
            [jnp.where(lane == g, grad, 0.0).astype(BF) for g in range(per)], axis=0
        )
        skew_ref[...] = dot_nt(stacked, back_ref[groups * KL :, u * TILE : (u + 1) * TILE])
        for g in range(per):
            rolled = pltpu.roll(skew_ref[g * KL : (g + 1) * KL, :], 0, 1, stride=1, stride_axis=0)
            lags.append(jnp.sum(rolled, axis=0, keepdims=True))
    if groups < GW:
        lags.append(jnp.zeros((GW - groups, WIN), F32))
    sums = pltpu.roll(jnp.concatenate(lags, axis=0), WIN - (KL - 1), 1)
    long = sums[:, :KL].astype(BF)
    for u in range(channels // TILE):
        out_ref[u, 32:AUX, :] = long


def sum_body(copies, in_ref, out_ref):
    total = in_ref[0].astype(F32)
    for s in range(1, in_ref.shape[0]):
        total = total + in_ref[s].astype(F32)
    value = total.astype(BF)
    for s in range(copies):
        out_ref[s] = value


def merge_body(sums_ref, *refs):
    grads, out_ref = refs[:-1], refs[-1]
    halves = sums_ref.shape[0] // len(grads)
    for p, ref in enumerate(grads):
        out_ref[p, :KL, :] = ref[...]
        for u in range(halves):
            out_ref[p, KL:, u * TILE : (u + 1) * TILE] = sums_ref[p * halves + u]


def spread_body(slices, width, in_ref, grad_ref, short_ref, long_ref):
    planes = in_ref.shape[0]
    matrix = swap_matrix(width)
    grad_ref[...] = join_owned([in_ref[z, :KL] for z in range(planes)], width, matrix).astype(BF)
    short = join_owned([in_ref[z, KL : KL + 32] for z in range(planes)], width, matrix)
    for j in range(KS):
        short_ref[j, 0:3, :] = short[3 * j : 3 * j + 3]
    per = width // GW
    groups = slices * per
    stacked = jnp.concatenate(
        [in_ref[z, KL + 32 : KL + 32 + groups, :KL] for z in range(planes)], axis=0
    )
    mover = filter_rows(slices, planes, per)
    long_ref[...] = lax.dot_general(
        mover, stacked, (((0,), (0,)), ((), ())), preferred_element_type=F32
    )


def from_next(x, by):
    size = lax.axis_size("seq")
    return lax.ppermute(x, "seq", [(i, i - by) for i in range(by, size)])


def from_before(x, by):
    size = lax.axis_size("seq")
    return lax.ppermute(x, "seq", [(i, i + by) for i in range(size - by)])


def per_device(layer_inputs, out_grad, short_weights, long_filters, out_weights):
    planes = lax.axis_size("pipe")
    blocks = lax.axis_size("seq")
    depth = out_weights.shape[2]
    half = out_grad.shape[1]
    width = depth // planes
    slices = half // depth
    owned = slices * width
    groups = owned // GW
    tokens = out_grad.shape[0]
    dims = long_filters.shape[1]

    tp_index = lax.axis_index("tp").astype(jnp.int32).reshape(1)
    own_rows = layer_inputs[0]
    swapped = lax.ppermute(own_rows, "tp", [(0, 1), (1, 0)])
    packed = pl.pallas_call(
        functools.partial(pack_body, planes, slices, width),
        out_shape=shape((planes, tokens + depth + AUX, owned), BF),
        in_specs=[pl.BlockSpec(memory_space=pltpu.SMEM)]
        + [pl.BlockSpec(memory_space=pltpu.VMEM)] * 5,
        compiler_params=pltpu.CompilerParams(vmem_limit_bytes=VMEM_LIMIT),
        interpret=INTERPRET,
    )(
        tp_index,
        out_weights[0].reshape(slices, planes, width, depth),
        short_weights[0],
        long_filters[0],
        own_rows,
        swapped,
    )
    packed = lax.all_to_all(packed, "pipe", 0, 0, tiled=True)
    top = planes - 1

    before2 = from_before(packed[:, tokens - PAD : tokens], 2)
    after = from_next(packed[:, :PAD], 1)

    def whole(x):
        return pl.BlockSpec(x.shape, lambda i: (0,) * len(x.shape))

    def plane(x, p, count, at=0):
        return pl.BlockSpec((None, count, x.shape[2]), lambda i, p=p, at=at: (p, at, 0))

    def own_block(p):
        return plane(packed, p, tokens)

    def aux_block(p):
        return plane(packed, p, AUX, (tokens + depth) // AUX)

    def recomputed(p, before, at):
        results = (shape((4 * REACH, owned), F32), shape((groups * KL + WIN, owned), BF))
        return call(
            functools.partial(recompute_body, groups),
            results,
            packed,
            before,
            before2,
            after,
            packed,
            grid=(1,),
            in_specs=[
                own_block(p),
                plane(before, at, tokens),
                plane(before2, p, PAD),
                plane(after, p, PAD),
                aux_block(p),
            ],
            out_specs=tuple(whole(r) for r in results),
            scratch_shapes=[
                pltpu.VMEM((2 * KL + 2 * PAD, owned), F32),
                pltpu.VMEM((groups * KL, WIN), BF),
            ],
        )

    def gathered(source, first, last):
        pieces = lax.all_gather(source[first : last + 1, tokens : tokens + depth], "seq", axis=0)
        return pieces.reshape(blocks, last + 1 - first, planes, width, owned)

    def copied(p):
        copies = jnp.broadcast_to(packed[p, tokens : tokens + depth][None], (blocks, depth, owned))
        pieces = lax.all_to_all(copies, "seq", 0, 0, tiled=True)
        return pieces.reshape(blocks, 1, planes, width, owned)

    starts = call(
        functools.partial(shuffle_body, planes, width),
        shape((planes, tokens, owned), BF),
        out_grad,
    )
    grad = lax.dynamic_index_in_dim(starts, lax.axis_index("pipe"), 0, keepdims=False)
    swap = [(0, 1), (1, 0)]
    other = lax.ppermute(grad, "tp", swap)

    before = {top: (from_before(packed[top:, :tokens], 1), 0)}
    saved = {top: recomputed(top, *before[top])}
    first_weights, saved[top], source, grad, other = lax.optimization_barrier(
        (copied(top), saved[top], packed, grad, other)
    )
    others = from_before(source[:top, :tokens], 1)
    before.update({p: (others, p) for p in range(top)})
    weights = {top: (first_weights, 0)}
    last = planes - 2
    for size in (1, 2, 2, planes):
        first = max(0, last - size + 1)
        if last >= first:
            group = gathered(packed, first, last)
            weights.update({p: (group, p - first) for p in range(first, last + 1)})
        last = first - 1

    def filter_sums(p, operands, sums):
        halves = owned // TILE
        result = shape((planes * halves, AUX, TILE), BF)
        earlier, at = before[p]
        specs = [whole(x) for x in operands]
        specs += [own_block(p), plane(earlier, at, PAD, tokens // PAD - 1)]
        operands = [*operands, packed, earlier]
        aliases = {}
        if sums is not None:
            aliases = {len(operands): 0}
            operands.append(sums)
            specs.append(pl.BlockSpec(memory_space=pl.ANY))
        return call(
            functools.partial(filters_body, groups),
            result,
            *operands,
            grid=(1,),
            in_specs=specs,
            out_specs=pl.BlockSpec((halves, AUX, TILE), lambda i, p=p: (p, 0, 0)),
            input_output_aliases=aliases,
            scratch_shapes=[
                pltpu.VMEM((KL + PAD, owned), F32),
                pltpu.VMEM((TILE // GW * KL, WIN), F32),
            ],
        )

    outs = [None] * planes
    sums = None
    late = None
    for p in range(planes - 1, -1, -1):
        group, at = weights[p]
        features, back = saved[p]
        if p + 1 < planes:
            other = lax.ppermute(grad, "tp", swap)
        partial = pl.pallas_call(
            project_body,
            out_shape=shape((planes, tokens, owned), BF),
            grid_spec=pltpu.PrefetchScalarGridSpec(
                num_scalar_prefetch=1,
                grid=(2,),
                in_specs=[
                    pl.BlockSpec((tokens, owned), lambda z, t: (0, 0)),
                    pl.BlockSpec((tokens, owned), lambda z, t: (0, 0)),
                    pl.BlockSpec(
                        (blocks, 1, planes // 2, width, owned), lambda z, t, at=at: (0, at, z, 0, 0)
                    ),
                ],
                out_specs=pl.BlockSpec((planes // 2, tokens, owned), lambda z, t: (z, 0, 0)),
            ),
            compiler_params=pltpu.CompilerParams(vmem_limit_bytes=VMEM_LIMIT),
            interpret=INTERPRET,
        )(tp_index, grad, other, group)
        parts = lax.all_to_all(partial, "pipe", 0, 0, tiled=True)
        send, dgate, early = call(
            gate_body,
            (
                shape((KL + PAD, owned), BF),
                shape((KL, owned), BF),
                shape((PAD, owned), BF),
            ),
            parts,
            features,
        )
        near = from_next(send, 1)
        far = from_next(early, 2)
        if late is not None:
            send, late[0] = lax.optimization_barrier((send, late[0]))
            sums = filter_sums(p + 1, late, sums)
            near, sums = lax.optimization_barrier((near, sums))
        if p > 0:
            earlier, at = before[p - 1]
            send, earlier = lax.optimization_barrier((send, earlier))
            saved[p - 1] = recomputed(p - 1, earlier, at)
            near, saved[p - 1] = lax.optimization_barrier((near, saved[p - 1]))
        results = (shape((KL, owned), BF), shape((3 * KL, owned), F32))
        operands = (send, dgate, near, far, features, back, packed, grad)
        new_grad, trail = call(
            functools.partial(finish_body, groups),
            results,
            *operands,
            grid=(1,),
            in_specs=[aux_block(p) if x is packed else whole(x) for x in operands],
            out_specs=tuple(whole(r) for r in results),
            scratch_shapes=[pltpu.VMEM((REACH, owned), F32)] * 3,
        )
        late = [trail, send, back]
        outs[p] = new_grad
        grad = new_grad

    sums = filter_sums(0, late, sums)
    exchanged = lax.all_to_all(sums, "seq", 0, 0, tiled=True)
    summed = call(
        functools.partial(sum_body, blocks), shape((blocks, AUX, TILE), BF), exchanged
    )
    summed = lax.all_to_all(summed, "seq", 0, 0, tiled=True)
    merged = call(merge_body, shape((planes, tokens + AUX, owned), BF), summed, *outs)
    results = lax.all_to_all(merged, "pipe", 0, 0, tiled=True)
    input_grad, short_result, long_result = call(
        functools.partial(spread_body, slices, width),
        (shape((tokens, half), BF), shape((KS, 8, half), F32), shape((dims, KL), F32)),
        results,
    )
    return input_grad[None], short_result[None, :, :3], long_result[None]


def solution(mesh):
    in_specs = (
        P("pipe", ("seq", "tp"), None),
        P("seq", "tp"),
        P("pipe", None, None, "tp"),
        P("pipe", "tp", None),
        P("pipe", "tp", "seq"),
    )
    out_specs = (P("pipe", "seq", "tp"), P("pipe", None, None, "tp"), P("pipe", "tp", None))
    return jax.shard_map(
        per_device, mesh=mesh, in_specs=in_specs, out_specs=out_specs, check_vma=False
    )
```

```python
import functools

import jax
import jax.numpy as jnp
from jax import lax
from jax.experimental import pallas as pl
from jax.experimental.pallas import tpu as pltpu
from jax.sharding import PartitionSpec as P

KL = 128
KS = 7
TILE = 128
GW = 16
AUX = 48
EDGE = 8
REACH = KL + EDGE
PAD = 16
WIN = 2 * KL
BF = jnp.bfloat16
F32 = jnp.float32
VMEM_LIMIT = 24 * 1024 * 1024
INTERPRET = False


def call(body, out_shape, *args, **kwargs):
    return pl.pallas_call(
        body,
        out_shape=out_shape,
        compiler_params=pltpu.CompilerParams(vmem_limit_bytes=VMEM_LIMIT),
        interpret=INTERPRET,
        **kwargs,
    )(*args)


def shape(dims, dtype):
    return jax.ShapeDtypeStruct(dims, dtype)


def dot(a, b):
    return jnp.dot(a, b, preferred_element_type=F32)


def dot_nt(a, b):
    return lax.dot_general(a, b, (((1,), (1,)), ((), ())), preferred_element_type=F32)


def swap_matrix(width):
    size = TILE // width
    n = size * TILE
    row = lax.broadcasted_iota(jnp.int32, (n, n), 0)
    col = lax.broadcasted_iota(jnp.int32, (n, n), 1)
    a, b, j = row // TILE, (row // width) % size, row % width
    return (col == b * TILE + a * width + j).astype(F32).astype(BF)


def split_owned(x, planes, width, matrix):
    step = planes * width
    slices = x.shape[1] // step
    size = TILE // width
    pieces = [[None] * (slices // size) for _ in range(planes)]
    for a in range(slices // size):
        for b in range(planes // size):
            tiles = [
                x[:, (a * size + i) * step + b * TILE : (a * size + i) * step + (b + 1) * TILE]
                for i in range(size)
            ]
            moved = dot(jnp.concatenate(tiles, axis=1), matrix).astype(BF)
            for i in range(size):
                pieces[b * size + i][a] = moved[:, i * TILE : (i + 1) * TILE]
    return [jnp.concatenate(p, axis=1) for p in pieces]


def join_owned(parts, width, matrix):
    planes = len(parts)
    size = TILE // width
    slices = parts[0].shape[1] // width
    out = [[None] * (planes // size) for _ in range(slices)]
    for a in range(slices // size):
        for b in range(planes // size):
            tiles = [parts[b * size + i][:, a * TILE : (a + 1) * TILE] for i in range(size)]
            moved = dot(jnp.concatenate(tiles, axis=1), matrix)
            for i in range(size):
                out[a * size + i][b] = moved[:, i * TILE : (i + 1) * TILE]
    return jnp.concatenate([jnp.concatenate(o, axis=1) for o in out], axis=1)


def filter_rows(slices, planes, per):
    n = slices * planes * per
    row = lax.broadcasted_iota(jnp.int32, (n, n), 0)
    col = lax.broadcasted_iota(jnp.int32, (n, n), 1)
    z, k, g = row // (slices * per), (row // per) % slices, row % per
    return (col == k * planes * per + z * per + g).astype(F32).astype(BF)


def pack_body(
    planes, slices, width, tp_ref, w_hbm, sw_ref, lf_ref, x_hbm, other_hbm, out_ref,
    w_ref, x_ref, other_ref, sems,
):
    pairs = ((x_hbm, x_ref), (other_hbm, other_ref), (w_hbm, w_ref))
    copies = [pltpu.make_async_copy(a, b, sems.at[i]) for i, (a, b) in enumerate(pairs)]
    for copy in copies:
        copy.start()
    owned = slices * width
    depth = planes * width
    half = slices * depth
    count = x_ref.shape[0]
    matrix = swap_matrix(width)
    tp = tp_ref[0]
    start = pl.multiple_of(tp * half, TILE)
    for copy, source, place in ((copies[0], x_ref, tp), (copies[1], other_ref, 1 - tp)):
        copy.wait()
        pieces = split_owned(source[:, pl.ds(start, half)], planes, width, matrix)
        at = pl.multiple_of(place * count, PAD)
        for z in range(planes):
            out_ref[z, pl.ds(at, count), :] = pieces[z]
    copies[2].wait()
    for z in range(planes):
        block = w_ref[:, z].reshape(owned, depth)
        turned = block.astype(F32).T.astype(BF)
        low = KL + z * width
        out_ref[:, low : low + width, :] = turned.reshape(planes, width, owned)
    base = KL + depth
    taps = [sw_ref[j].astype(F32) for j in range(KS)]
    taps.append(jnp.zeros((32 - 3 * KS, half), F32))
    taps = split_owned(jnp.concatenate(taps, axis=0).astype(BF), planes, width, matrix)
    per = width // GW
    filters = dot(filter_rows(slices, planes, per), lf_ref[...]).astype(BF)
    groups = slices * per
    for z in range(planes):
        out_ref[z, base : base + 32, :] = taps[z]
        out_ref[z, base + 32 : base + AUX, :] = jnp.zeros((GW, owned), BF)
        out_ref[z, base + 32 : base + 32 + groups, :KL] = filters[z * groups : (z + 1) * groups]


def shuffle_body(planes, width, x_ref, out_ref):
    pieces = split_owned(x_ref[...], planes, width, swap_matrix(width))
    for z in range(planes):
        out_ref[z] = pieces[z]


def grouped(toeplitz, rows_per, source, groups):
    channels = source.shape[1]
    tiles = []
    for u in range(channels // TILE):
        per = TILE // GW
        full = dot(toeplitz[u * per * rows_per : (u + 1) * per * rows_per], source[:, u * TILE : (u + 1) * TILE])
        lane = lax.broadcasted_iota(jnp.int32, (rows_per, TILE), 1) // GW
        merged = full[:rows_per]
        for g in range(1, per):
            merged = jnp.where(lane == g, full[g * rows_per : (g + 1) * rows_per], merged)
        tiles.append(merged)
    return jnp.concatenate(tiles, axis=1)


def edge_rows(ref, groups):
    return jnp.concatenate(
        [ref[g * KL + KL - PAD : (g + 1) * KL, :] for g in range(groups)], axis=0
    )


def recompute_body(
    groups, own_ref, prev_ref, prev2_ref, next_ref, aux_ref, features_ref, back_ref, rows_ref, band_ref,
):
    rows_ref[0:PAD, :] = prev2_ref[...].astype(F32)
    rows_ref[PAD : PAD + KL, :] = prev_ref[...].astype(F32)
    rows_ref[PAD + KL : PAD + 2 * KL, :] = own_ref[...].astype(F32)
    rows_ref[PAD + 2 * KL :, :] = next_ref[...].astype(F32)
    taps = aux_ref[0:32, :].astype(F32)

    def feature(f, first, count):
        start = PAD + KL + first
        total = taps[f : f + 1] * rows_ref[start : start + count, :]
        for j in range(1, KS):
            total = total + taps[3 * j + f : 3 * j + f + 1] * rows_ref[start - j : start - j + count, :]
        return total

    features_ref[0:REACH, :] = feature(0, 0, REACH)
    key_tail = feature(1, 0, REACH)
    value_tail = feature(2, 0, REACH)
    features_ref[REACH : 2 * REACH, :] = key_tail
    features_ref[2 * REACH : 3 * REACH, :] = value_tail
    kv = jnp.concatenate([feature(1, -KL, KL) * feature(2, -KL, KL), key_tail * value_tail], axis=0)
    window = kv[:WIN].astype(BF)
    late = kv[EDGE : EDGE + WIN].astype(BF)

    filters = aux_ref[32 : 32 + groups, :KL]
    tap = lax.broadcasted_iota(jnp.int32, (KL, WIN), 0)
    lane = lax.broadcasted_iota(jnp.int32, (KL, WIN), 1)
    ahead = dot(filters, (lane == KL - tap).astype(F32).astype(BF))
    behind = dot(filters, (lane == tap).astype(F32).astype(BF))
    for g in range(groups):
        wide = jnp.broadcast_to(ahead[g : g + 1], (KL, WIN))
        band_ref[g * KL : (g + 1) * KL, :] = pltpu.roll(wide, 0, 1, stride=1, stride_axis=0).astype(BF)
        wide = jnp.broadcast_to(behind[g : g + 1], (KL, WIN))
        back_ref[g * KL : (g + 1) * KL, :] = pltpu.roll(wide, 0, 1, stride=1, stride_axis=0).astype(BF)
    features_ref[3 * REACH : 3 * REACH + KL, :] = grouped(band_ref, KL, window, groups)
    features_ref[3 * REACH + KL :, :] = grouped(edge_rows(band_ref, groups), PAD, late, groups)[PAD - EDGE :]
    source = lax.broadcasted_iota(jnp.int32, (WIN, WIN), 0)
    target = lax.broadcasted_iota(jnp.int32, (WIN, WIN), 1)
    mirror = (source + target == WIN - 1).astype(F32).astype(BF)
    back_ref[groups * KL :, :] = dot(mirror, window).astype(BF)


def project_body(tp_ref, own_ref, other_ref, w_ref, out_ref):
    first = tp_ref[0] == 0
    own, other = own_ref[...], other_ref[...]
    rows = jnp.concatenate([jnp.where(first, own, other), jnp.where(first, other, own)], axis=1)
    slices, _, count, width, owned = w_ref.shape
    for z in range(count):
        out_ref[z] = dot(rows, w_ref[:, 0, z].reshape(slices * width, owned)).astype(BF)


def gate_body(parts_ref, features_ref, send_ref, dgate_ref, early_ref):
    total = parts_ref[0].astype(F32)
    for z in range(1, parts_ref.shape[0]):
        total = total + parts_ref[z].astype(F32)
    dgate = total.astype(BF)
    dmixed = (dgate.astype(F32) * features_ref[0:KL, :]).astype(BF)
    send_ref[0:KL, :] = dmixed
    send_ref[KL:, :] = dgate[:PAD]
    dgate_ref[...] = dgate
    early_ref[...] = dmixed[:PAD]


def finish_body(
    groups, send_ref, dgate_ref, near_ref, far_ref, features_ref, back_ref, aux_ref, grad_ref,
    out_ref, trail_ref, d0_ref, d1_ref, d2_ref,
):
    rows = jnp.concatenate(
        [send_ref[0:KL, :], near_ref[0:KL, :], far_ref[...]], axis=0
    )
    window = rows[:WIN]
    late = rows.astype(F32)[EDGE : EDGE + WIN].astype(BF)
    main = grouped(back_ref, KL, window, groups)
    tail = grouped(edge_rows(back_ref, groups), PAD, late, groups)[PAD - EDGE :]
    key, value, mixed = REACH, 2 * REACH, 3 * REACH
    d0_ref[0:KL, :] = dgate_ref[...].astype(F32) * features_ref[mixed : mixed + KL, :]
    d0_ref[KL:, :] = near_ref[KL:, :].astype(F32)[:EDGE] * features_ref[mixed + KL :, :]
    d1_ref[0:KL, :] = main * features_ref[value : value + KL, :]
    d1_ref[KL:, :] = tail * features_ref[value + KL : mixed, :]
    d2_ref[0:KL, :] = main * features_ref[key : key + KL, :]
    d2_ref[KL:, :] = tail * features_ref[key + KL : value, :]
    taps = aux_ref[0:32, :].astype(F32)
    total = grad_ref[...].astype(F32)
    for f, ref in enumerate((d0_ref, d1_ref, d2_ref)):
        trail_ref[f * KL : (f + 1) * KL, :] = ref[0:KL, :]
        for j in range(KS):
            total = total + taps[3 * j + f : 3 * j + f + 1] * ref[j : j + KL, :]
    out_ref[...] = total.astype(BF)


def filters_body(
    groups, trail_ref, send_ref, back_ref, own_ref, prev_ref, *refs,
):
    out_ref, rows_ref, skew_ref = refs[-3:]
    channels = own_ref.shape[1]
    rows_ref[0:PAD, :] = prev_ref[...].astype(F32)
    rows_ref[PAD:, :] = own_ref[...].astype(F32)
    sums = []
    for j in range(KS):
        source = rows_ref[PAD - j : PAD - j + KL, :]
        for f in range(3):
            grads = trail_ref[f * KL : (f + 1) * KL, :]
            sums.append(jnp.sum(grads * source, axis=0, keepdims=True))
    sums.append(jnp.zeros((32 - 3 * KS, channels), F32))
    short = jnp.concatenate(sums, axis=0).astype(BF)
    for u in range(channels // TILE):
        out_ref[u, 0:32, :] = short[:, u * TILE : (u + 1) * TILE]
    lags = []
    per = TILE // GW
    lane = lax.broadcasted_iota(jnp.int32, (KL, TILE), 1) // GW
    for u in range(channels // TILE):
        grad = send_ref[0:KL, u * TILE : (u + 1) * TILE].astype(F32)
        stacked = jnp.concatenate(
            [jnp.where(lane == g, grad, 0.0).astype(BF) for g in range(per)], axis=0
        )
        skew_ref[...] = dot_nt(stacked, back_ref[groups * KL :, u * TILE : (u + 1) * TILE])
        for g in range(per):
            rolled = pltpu.roll(skew_ref[g * KL : (g + 1) * KL, :], 0, 1, stride=1, stride_axis=0)
            lags.append(jnp.sum(rolled, axis=0, keepdims=True))
    if groups < GW:
        lags.append(jnp.zeros((GW - groups, WIN), F32))
    sums = pltpu.roll(jnp.concatenate(lags, axis=0), WIN - (KL - 1), 1)
    long = sums[:, :KL].astype(BF)
    for u in range(channels // TILE):
        out_ref[u, 32:AUX, :] = long


def sum_body(copies, in_ref, out_ref):
    total = in_ref[0].astype(F32)
    for s in range(1, in_ref.shape[0]):
        total = total + in_ref[s].astype(F32)
    value = total.astype(BF)
    for s in range(copies):
        out_ref[s] = value


def merge_body(sums_ref, *refs):
    grads, out_ref = refs[:-1], refs[-1]
    halves = sums_ref.shape[0] // len(grads)
    for p, ref in enumerate(grads):
        out_ref[p, :KL, :] = ref[...]
        for u in range(halves):
            out_ref[p, KL:, u * TILE : (u + 1) * TILE] = sums_ref[p * halves + u]


def spread_body(slices, width, in_ref, grad_ref, short_ref, long_ref):
    planes = in_ref.shape[0]
    matrix = swap_matrix(width)
    grad_ref[...] = join_owned([in_ref[z, :KL] for z in range(planes)], width, matrix).astype(BF)
    short = join_owned([in_ref[z, KL : KL + 32] for z in range(planes)], width, matrix)
    for j in range(KS):
        short_ref[j, 0:3, :] = short[3 * j : 3 * j + 3]
    per = width // GW
    groups = slices * per
    stacked = jnp.concatenate(
        [in_ref[z, KL + 32 : KL + 32 + groups, :KL] for z in range(planes)], axis=0
    )
    mover = filter_rows(slices, planes, per)
    long_ref[...] = lax.dot_general(
        mover, stacked, (((0,), (0,)), ((), ())), preferred_element_type=F32
    )


def from_next(x, by):
    size = lax.axis_size("seq")
    return lax.ppermute(x, "seq", [(i, i - by) for i in range(by, size)])


def from_before(x, by):
    size = lax.axis_size("seq")
    return lax.ppermute(x, "seq", [(i, i + by) for i in range(size - by)])


def per_device(layer_inputs, out_grad, short_weights, long_filters, out_weights):
    planes = lax.axis_size("pipe")
    blocks = lax.axis_size("seq")
    depth = out_weights.shape[2]
    half = out_grad.shape[1]
    width = depth // planes
    slices = half // depth
    owned = slices * width
    groups = owned // GW
    tokens = out_grad.shape[0]
    dims = long_filters.shape[1]

    tp_index = lax.axis_index("tp").astype(jnp.int32).reshape(1)
    own_rows = layer_inputs[0]
    swapped = lax.ppermute(own_rows, "tp", [(0, 1), (1, 0)])
    packed = pl.pallas_call(
        functools.partial(pack_body, planes, slices, width),
        out_shape=shape((planes, tokens + depth + AUX, owned), BF),
        in_specs=[
            pl.BlockSpec(memory_space=pltpu.SMEM),
            pl.BlockSpec(memory_space=pl.ANY),
            pl.BlockSpec(memory_space=pltpu.VMEM),
            pl.BlockSpec(memory_space=pltpu.VMEM),
            pl.BlockSpec(memory_space=pl.ANY),
            pl.BlockSpec(memory_space=pl.ANY),
        ],
        scratch_shapes=[
            pltpu.VMEM((slices, planes, width, depth), BF),
            pltpu.VMEM(own_rows.shape, BF),
            pltpu.VMEM(own_rows.shape, BF),
            pltpu.SemaphoreType.DMA((3,)),
        ],
        compiler_params=pltpu.CompilerParams(vmem_limit_bytes=VMEM_LIMIT),
        interpret=INTERPRET,
    )(
        tp_index,
        out_weights[0].reshape(slices, planes, width, depth),
        short_weights[0],
        long_filters[0],
        own_rows,
        swapped,
    )
    packed = lax.all_to_all(packed, "pipe", 0, 0, tiled=True)
    top = planes - 1

    before2 = from_before(packed[:, tokens - PAD : tokens], 2)
    after = from_next(packed[:, :PAD], 1)

    def whole(x):
        return pl.BlockSpec(x.shape, lambda i: (0,) * len(x.shape))

    def plane(x, p, count, at=0):
        return pl.BlockSpec((None, count, x.shape[2]), lambda i, p=p, at=at: (p, at, 0))

    def own_block(p):
        return plane(packed, p, tokens)

    def aux_block(p):
        return plane(packed, p, AUX, (tokens + depth) // AUX)

    def recomputed(p, before, at):
        results = (shape((4 * REACH, owned), F32), shape((groups * KL + WIN, owned), BF))
        return call(
            functools.partial(recompute_body, groups),
            results,
            packed,
            before,
            before2,
            after,
            packed,
            grid=(1,),
            in_specs=[
                own_block(p),
                plane(before, at, tokens),
                plane(before2, p, PAD),
                plane(after, p, PAD),
                aux_block(p),
            ],
            out_specs=tuple(whole(r) for r in results),
            scratch_shapes=[
                pltpu.VMEM((2 * KL + 2 * PAD, owned), F32),
                pltpu.VMEM((groups * KL, WIN), BF),
            ],
        )

    def gathered(source, first, last):
        pieces = lax.all_gather(source[first : last + 1, tokens : tokens + depth], "seq", axis=0)
        return pieces.reshape(blocks, last + 1 - first, planes, width, owned)

    def copied(p):
        copies = jnp.broadcast_to(packed[p, tokens : tokens + depth][None], (blocks, depth, owned))
        pieces = lax.all_to_all(copies, "seq", 0, 0, tiled=True)
        return pieces.reshape(blocks, 1, planes, width, owned)

    starts = call(
        functools.partial(shuffle_body, planes, width),
        shape((planes, tokens, owned), BF),
        out_grad,
    )
    grad = lax.dynamic_index_in_dim(starts, lax.axis_index("pipe"), 0, keepdims=False)
    swap = [(0, 1), (1, 0)]
    other = lax.ppermute(grad, "tp", swap)

    before = {top: (from_before(packed[top:, :tokens], 1), 0)}
    saved = {top: recomputed(top, *before[top])}
    first_weights, saved[top], source, grad, other = lax.optimization_barrier(
        (copied(top), saved[top], packed, grad, other)
    )
    others = from_before(source[:top, :tokens], 1)
    before.update({p: (others, p) for p in range(top)})
    weights = {top: (first_weights, 0)}
    last = planes - 2
    for size in (2, 2, planes):
        first = max(0, last - size + 1)
        if last >= first:
            group = gathered(packed, first, last)
            weights.update({p: (group, p - first) for p in range(first, last + 1)})
        last = first - 1

    def filter_sums(p, operands, sums):
        halves = owned // TILE
        result = shape((planes * halves, AUX, TILE), BF)
        earlier, at = before[p]
        specs = [whole(x) for x in operands]
        specs += [own_block(p), plane(earlier, at, PAD, tokens // PAD - 1)]
        operands = [*operands, packed, earlier]
        aliases = {}
        if sums is not None:
            aliases = {len(operands): 0}
            operands.append(sums)
            specs.append(pl.BlockSpec(memory_space=pl.ANY))
        return call(
            functools.partial(filters_body, groups),
            result,
            *operands,
            grid=(1,),
            in_specs=specs,
            out_specs=pl.BlockSpec((halves, AUX, TILE), lambda i, p=p: (p, 0, 0)),
            input_output_aliases=aliases,
            scratch_shapes=[
                pltpu.VMEM((KL + PAD, owned), F32),
                pltpu.VMEM((TILE // GW * KL, WIN), F32),
            ],
        )

    outs = [None] * planes
    sums = None
    late = None
    for p in range(planes - 1, -1, -1):
        group, at = weights[p]
        features, back = saved[p]
        if p + 1 < planes:
            other = lax.ppermute(grad, "tp", swap)
        partial = pl.pallas_call(
            project_body,
            out_shape=shape((planes, tokens, owned), BF),
            grid_spec=pltpu.PrefetchScalarGridSpec(
                num_scalar_prefetch=1,
                grid=(2,),
                in_specs=[
                    pl.BlockSpec((tokens, owned), lambda z, t: (0, 0)),
                    pl.BlockSpec((tokens, owned), lambda z, t: (0, 0)),
                    pl.BlockSpec(
                        (blocks, 1, planes // 2, width, owned), lambda z, t, at=at: (0, at, z, 0, 0)
                    ),
                ],
                out_specs=pl.BlockSpec((planes // 2, tokens, owned), lambda z, t: (z, 0, 0)),
            ),
            compiler_params=pltpu.CompilerParams(vmem_limit_bytes=VMEM_LIMIT),
            interpret=INTERPRET,
        )(tp_index, grad, other, group)
        parts = lax.all_to_all(partial, "pipe", 0, 0, tiled=True)
        send, dgate, early = call(
            gate_body,
            (
                shape((KL + PAD, owned), BF),
                shape((KL, owned), BF),
                shape((PAD, owned), BF),
            ),
            parts,
            features,
        )
        near = from_next(send, 1)
        far = from_next(early, 2)
        if late is not None:
            send, late[0] = lax.optimization_barrier((send, late[0]))
            sums = filter_sums(p + 1, late, sums)
            near, sums = lax.optimization_barrier((near, sums))
        if 0 < p < top - 1 and weights[p - 1][0] is not group:
            near, fetched = lax.optimization_barrier((near, weights[p - 1][0]))
            weights.update(
                {q: (fetched, i) for q, (g, i) in weights.items() if g is weights[p - 1][0]}
            )
        if p > 0:
            earlier, at = before[p - 1]
            send, earlier = lax.optimization_barrier((send, earlier))
            saved[p - 1] = recomputed(p - 1, earlier, at)
            near, saved[p - 1] = lax.optimization_barrier((near, saved[p - 1]))
        results = (shape((KL, owned), BF), shape((3 * KL, owned), F32))
        operands = (send, dgate, near, far, features, back, packed, grad)
        new_grad, trail = call(
            functools.partial(finish_body, groups),
            results,
            *operands,
            grid=(1,),
            in_specs=[aux_block(p) if x is packed else whole(x) for x in operands],
            out_specs=tuple(whole(r) for r in results),
            scratch_shapes=[pltpu.VMEM((REACH, owned), F32)] * 3,
        )
        late = [trail, send, back]
        outs[p] = new_grad
        grad = new_grad

    sums = filter_sums(0, late, sums)
    exchanged = lax.all_to_all(sums, "seq", 0, 0, tiled=True)
    summed = call(
        functools.partial(sum_body, blocks), shape((blocks, AUX, TILE), BF), exchanged
    )
    summed = lax.all_to_all(summed, "seq", 0, 0, tiled=True)
    merged = call(merge_body, shape((planes, tokens + AUX, owned), BF), summed, *outs)
    results = lax.all_to_all(merged, "pipe", 0, 0, tiled=True)
    input_grad, short_result, long_result = call(
        functools.partial(spread_body, slices, width),
        (shape((tokens, half), BF), shape((KS, 8, half), F32), shape((dims, KL), F32)),
        results,
    )
    return input_grad[None], short_result[None, :, :3], long_result[None]


def solution(mesh):
    in_specs = (
        P("pipe", ("seq", "tp"), None),
        P("seq", "tp"),
        P("pipe", None, None, "tp"),
        P("pipe", "tp", None),
        P("pipe", "tp", "seq"),
    )
    out_specs = (P("pipe", "seq", "tp"), P("pipe", None, None, "tp"), P("pipe", "tp", None))
    return jax.shard_map(
        per_device, mesh=mesh, in_specs=in_specs, out_specs=out_specs, check_vma=False
    )
```

```python
import functools

import jax
import jax.numpy as jnp
from jax import lax
from jax.experimental import pallas as pl
from jax.experimental.pallas import tpu as pltpu
from jax.sharding import PartitionSpec as P

KL = 128
KS = 7
TILE = 128
GW = 16
AUX = 48
EDGE = 8
REACH = KL + EDGE
PAD = 16
WIN = 2 * KL
BF = jnp.bfloat16
F32 = jnp.float32
VMEM_LIMIT = 24 * 1024 * 1024
INTERPRET = False


def call(body, out_shape, *args, **kwargs):
    return pl.pallas_call(
        body,
        out_shape=out_shape,
        compiler_params=pltpu.CompilerParams(vmem_limit_bytes=VMEM_LIMIT),
        interpret=INTERPRET,
        **kwargs,
    )(*args)


def shape(dims, dtype):
    return jax.ShapeDtypeStruct(dims, dtype)


def dot(a, b):
    return jnp.dot(a, b, preferred_element_type=F32)


def dot_nt(a, b):
    return lax.dot_general(a, b, (((1,), (1,)), ((), ())), preferred_element_type=F32)


def swap_matrix(width):
    size = TILE // width
    n = size * TILE
    row = lax.broadcasted_iota(jnp.int32, (n, n), 0)
    col = lax.broadcasted_iota(jnp.int32, (n, n), 1)
    a, b, j = row // TILE, (row // width) % size, row % width
    return (col == b * TILE + a * width + j).astype(F32).astype(BF)


def split_owned(x, planes, width, matrix):
    step = planes * width
    slices = x.shape[1] // step
    size = TILE // width
    pieces = [[None] * (slices // size) for _ in range(planes)]
    for a in range(slices // size):
        for b in range(planes // size):
            tiles = [
                x[:, (a * size + i) * step + b * TILE : (a * size + i) * step + (b + 1) * TILE]
                for i in range(size)
            ]
            moved = dot(jnp.concatenate(tiles, axis=1), matrix).astype(BF)
            for i in range(size):
                pieces[b * size + i][a] = moved[:, i * TILE : (i + 1) * TILE]
    return [jnp.concatenate(p, axis=1) for p in pieces]


def join_owned(parts, width, matrix):
    planes = len(parts)
    size = TILE // width
    slices = parts[0].shape[1] // width
    out = [[None] * (planes // size) for _ in range(slices)]
    for a in range(slices // size):
        for b in range(planes // size):
            tiles = [parts[b * size + i][:, a * TILE : (a + 1) * TILE] for i in range(size)]
            moved = dot(jnp.concatenate(tiles, axis=1), matrix)
            for i in range(size):
                out[a * size + i][b] = moved[:, i * TILE : (i + 1) * TILE]
    return jnp.concatenate([jnp.concatenate(o, axis=1) for o in out], axis=1)


def filter_rows(slices, planes, per):
    n = slices * planes * per
    row = lax.broadcasted_iota(jnp.int32, (n, n), 0)
    col = lax.broadcasted_iota(jnp.int32, (n, n), 1)
    z, k, g = row // (slices * per), (row // per) % slices, row % per
    return (col == k * planes * per + z * per + g).astype(F32).astype(BF)


def pack_body(planes, slices, width, w_ref, sw_ref, lf_ref, out_ref):
    owned = slices * width
    depth = planes * width
    half = slices * depth
    for z in range(planes):
        block = w_ref[:, z].reshape(owned, depth)
        turned = block.astype(F32).T.astype(BF)
        low = AUX + z * width
        out_ref[:, low : low + width, :] = turned.reshape(planes, width, owned)
    taps = [sw_ref[j].astype(F32) for j in range(KS)]
    taps.append(jnp.zeros((32 - 3 * KS, half), F32))
    taps = jnp.concatenate(taps, axis=0).astype(BF)
    taps = split_owned(taps, planes, width, swap_matrix(width))
    per = width // GW
    filters = dot(filter_rows(slices, planes, per), lf_ref[...]).astype(BF)
    groups = slices * per
    for z in range(planes):
        out_ref[z, 0:32, :] = taps[z]
        out_ref[z, 32:AUX, :] = jnp.zeros((GW, owned), BF)
        out_ref[z, 32 : 32 + groups, :KL] = filters[z * groups : (z + 1) * groups]


def scatter_body(planes, slices, width, tp_ref, x_ref, other_ref, out_ref):
    half = slices * planes * width
    count = x_ref.shape[0]
    matrix = swap_matrix(width)
    tp = tp_ref[0]
    start = pl.multiple_of(tp * half, TILE)
    for source, place in ((x_ref, tp), (other_ref, 1 - tp)):
        pieces = split_owned(source[:, pl.ds(start, half)], planes, width, matrix)
        at = pl.multiple_of(place * count, PAD)
        for z in range(planes):
            out_ref[z, pl.ds(at, count), :] = pieces[z]


def shuffle_body(planes, width, x_ref, out_ref):
    pieces = split_owned(x_ref[...], planes, width, swap_matrix(width))
    for z in range(planes):
        out_ref[z] = pieces[z]


def grouped(toeplitz, rows_per, source, groups):
    channels = source.shape[1]
    tiles = []
    for u in range(channels // TILE):
        per = TILE // GW
        full = dot(toeplitz[u * per * rows_per : (u + 1) * per * rows_per], source[:, u * TILE : (u + 1) * TILE])
        lane = lax.broadcasted_iota(jnp.int32, (rows_per, TILE), 1) // GW
        merged = full[:rows_per]
        for g in range(1, per):
            merged = jnp.where(lane == g, full[g * rows_per : (g + 1) * rows_per], merged)
        tiles.append(merged)
    return jnp.concatenate(tiles, axis=1)


def edge_rows(ref, groups):
    return jnp.concatenate(
        [ref[g * KL + KL - PAD : (g + 1) * KL, :] for g in range(groups)], axis=0
    )


def recompute_body(
    groups, own_ref, prev_ref, prev2_ref, next_ref, aux_ref, features_ref, back_ref, rows_ref, band_ref,
):
    rows_ref[0:PAD, :] = prev2_ref[...].astype(F32)
    rows_ref[PAD : PAD + KL, :] = prev_ref[...].astype(F32)
    rows_ref[PAD + KL : PAD + 2 * KL, :] = own_ref[...].astype(F32)
    rows_ref[PAD + 2 * KL :, :] = next_ref[...].astype(F32)
    taps = aux_ref[0:32, :].astype(F32)

    def feature(f, first, count):
        start = PAD + KL + first
        total = taps[f : f + 1] * rows_ref[start : start + count, :]
        for j in range(1, KS):
            total = total + taps[3 * j + f : 3 * j + f + 1] * rows_ref[start - j : start - j + count, :]
        return total

    features_ref[0:REACH, :] = feature(0, 0, REACH)
    key_tail = feature(1, 0, REACH)
    value_tail = feature(2, 0, REACH)
    features_ref[REACH : 2 * REACH, :] = key_tail
    features_ref[2 * REACH : 3 * REACH, :] = value_tail
    kv = jnp.concatenate([feature(1, -KL, KL) * feature(2, -KL, KL), key_tail * value_tail], axis=0)
    window = kv[:WIN].astype(BF)
    late = kv[EDGE : EDGE + WIN].astype(BF)

    filters = aux_ref[32 : 32 + groups, :KL]
    tap = lax.broadcasted_iota(jnp.int32, (KL, WIN), 0)
    lane = lax.broadcasted_iota(jnp.int32, (KL, WIN), 1)
    ahead = dot(filters, (lane == KL - tap).astype(F32).astype(BF))
    behind = dot(filters, (lane == tap).astype(F32).astype(BF))
    for g in range(groups):
        wide = jnp.broadcast_to(ahead[g : g + 1], (KL, WIN))
        band_ref[g * KL : (g + 1) * KL, :] = pltpu.roll(wide, 0, 1, stride=1, stride_axis=0).astype(BF)
        wide = jnp.broadcast_to(behind[g : g + 1], (KL, WIN))
        back_ref[g * KL : (g + 1) * KL, :] = pltpu.roll(wide, 0, 1, stride=1, stride_axis=0).astype(BF)
    features_ref[3 * REACH : 3 * REACH + KL, :] = grouped(band_ref, KL, window, groups)
    features_ref[3 * REACH + KL :, :] = grouped(edge_rows(band_ref, groups), PAD, late, groups)[PAD - EDGE :]
    source = lax.broadcasted_iota(jnp.int32, (WIN, WIN), 0)
    target = lax.broadcasted_iota(jnp.int32, (WIN, WIN), 1)
    mirror = (source + target == WIN - 1).astype(F32).astype(BF)
    back_ref[groups * KL :, :] = dot(mirror, window).astype(BF)


def project_body(tp_ref, own_ref, other_ref, w_ref, out_ref):
    first = tp_ref[0] == 0
    own, other = own_ref[...], other_ref[...]
    rows = jnp.concatenate([jnp.where(first, own, other), jnp.where(first, other, own)], axis=1)
    slices, _, count, width, owned = w_ref.shape
    for z in range(count):
        out_ref[z] = dot(rows, w_ref[:, 0, z].reshape(slices * width, owned)).astype(BF)


def gate_body(parts_ref, features_ref, send_ref, dgate_ref, early_ref):
    total = parts_ref[0].astype(F32)
    for z in range(1, parts_ref.shape[0]):
        total = total + parts_ref[z].astype(F32)
    dgate = total.astype(BF)
    dmixed = (dgate.astype(F32) * features_ref[0:KL, :]).astype(BF)
    send_ref[0:KL, :] = dmixed
    send_ref[KL:, :] = dgate[:PAD]
    dgate_ref[...] = dgate
    early_ref[...] = dmixed[:PAD]


def finish_body(
    groups, send_ref, dgate_ref, near_ref, far_ref, features_ref, back_ref, aux_ref, grad_ref,
    out_ref, trail_ref, d0_ref, d1_ref, d2_ref,
):
    rows = jnp.concatenate(
        [send_ref[0:KL, :], near_ref[0:KL, :], far_ref[...]], axis=0
    )
    window = rows[:WIN]
    late = rows.astype(F32)[EDGE : EDGE + WIN].astype(BF)
    main = grouped(back_ref, KL, window, groups)
    tail = grouped(edge_rows(back_ref, groups), PAD, late, groups)[PAD - EDGE :]
    key, value, mixed = REACH, 2 * REACH, 3 * REACH
    d0_ref[0:KL, :] = dgate_ref[...].astype(F32) * features_ref[mixed : mixed + KL, :]
    d0_ref[KL:, :] = near_ref[KL:, :].astype(F32)[:EDGE] * features_ref[mixed + KL :, :]
    d1_ref[0:KL, :] = main * features_ref[value : value + KL, :]
    d1_ref[KL:, :] = tail * features_ref[value + KL : mixed, :]
    d2_ref[0:KL, :] = main * features_ref[key : key + KL, :]
    d2_ref[KL:, :] = tail * features_ref[key + KL : value, :]
    taps = aux_ref[0:32, :].astype(F32)
    total = grad_ref[...].astype(F32)
    for f, ref in enumerate((d0_ref, d1_ref, d2_ref)):
        trail_ref[f * KL : (f + 1) * KL, :] = ref[0:KL, :]
        for j in range(KS):
            total = total + taps[3 * j + f : 3 * j + f + 1] * ref[j : j + KL, :]
    out_ref[...] = total.astype(BF)


def filters_body(
    groups, trail_ref, send_ref, back_ref, own_ref, prev_ref, *refs,
):
    out_ref, rows_ref, skew_ref = refs[-3:]
    channels = own_ref.shape[1]
    rows_ref[0:PAD, :] = prev_ref[...].astype(F32)
    rows_ref[PAD:, :] = own_ref[...].astype(F32)
    sums = []
    for j in range(KS):
        source = rows_ref[PAD - j : PAD - j + KL, :]
        for f in range(3):
            grads = trail_ref[f * KL : (f + 1) * KL, :]
            sums.append(jnp.sum(grads * source, axis=0, keepdims=True))
    sums.append(jnp.zeros((32 - 3 * KS, channels), F32))
    short = jnp.concatenate(sums, axis=0).astype(BF)
    for u in range(channels // TILE):
        out_ref[u, 0:32, :] = short[:, u * TILE : (u + 1) * TILE]
    lags = []
    per = TILE // GW
    lane = lax.broadcasted_iota(jnp.int32, (KL, TILE), 1) // GW
    for u in range(channels // TILE):
        grad = send_ref[0:KL, u * TILE : (u + 1) * TILE].astype(F32)
        stacked = jnp.concatenate(
            [jnp.where(lane == g, grad, 0.0).astype(BF) for g in range(per)], axis=0
        )
        skew_ref[...] = dot_nt(stacked, back_ref[groups * KL :, u * TILE : (u + 1) * TILE])
        for g in range(per):
            rolled = pltpu.roll(skew_ref[g * KL : (g + 1) * KL, :], 0, 1, stride=1, stride_axis=0)
            lags.append(jnp.sum(rolled, axis=0, keepdims=True))
    if groups < GW:
        lags.append(jnp.zeros((GW - groups, WIN), F32))
    sums = pltpu.roll(jnp.concatenate(lags, axis=0), WIN - (KL - 1), 1)
    long = sums[:, :KL].astype(BF)
    for u in range(channels // TILE):
        out_ref[u, 32:AUX, :] = long


def sum_body(copies, in_ref, out_ref):
    total = in_ref[0].astype(F32)
    for s in range(1, in_ref.shape[0]):
        total = total + in_ref[s].astype(F32)
    value = total.astype(BF)
    for s in range(copies):
        out_ref[s] = value


def merge_body(sums_ref, *refs):
    grads, out_ref = refs[:-1], refs[-1]
    halves = sums_ref.shape[0] // len(grads)
    for p, ref in enumerate(grads):
        out_ref[p, :KL, :] = ref[...]
        for u in range(halves):
            out_ref[p, KL:, u * TILE : (u + 1) * TILE] = sums_ref[p * halves + u]


def spread_body(slices, width, in_ref, grad_ref, short_ref, long_ref):
    planes = in_ref.shape[0]
    matrix = swap_matrix(width)
    grad_ref[...] = join_owned([in_ref[z, :KL] for z in range(planes)], width, matrix).astype(BF)
    short = join_owned([in_ref[z, KL : KL + 32] for z in range(planes)], width, matrix)
    for j in range(KS):
        short_ref[j, 0:3, :] = short[3 * j : 3 * j + 3]
    per = width // GW
    groups = slices * per
    stacked = jnp.concatenate(
        [in_ref[z, KL + 32 : KL + 32 + groups, :KL] for z in range(planes)], axis=0
    )
    mover = filter_rows(slices, planes, per)
    long_ref[...] = lax.dot_general(
        mover, stacked, (((0,), (0,)), ((), ())), preferred_element_type=F32
    )


def from_next(x, by):
    size = lax.axis_size("seq")
    return lax.ppermute(x, "seq", [(i, i - by) for i in range(by, size)])


def from_before(x, by):
    size = lax.axis_size("seq")
    return lax.ppermute(x, "seq", [(i, i + by) for i in range(size - by)])


def per_device(layer_inputs, out_grad, short_weights, long_filters, out_weights):
    planes = lax.axis_size("pipe")
    blocks = lax.axis_size("seq")
    depth = out_weights.shape[2]
    half = out_grad.shape[1]
    width = depth // planes
    slices = half // depth
    owned = slices * width
    groups = owned // GW
    tokens = out_grad.shape[0]
    dims = long_filters.shape[1]

    top = planes - 1
    tp_index = lax.axis_index("tp").astype(jnp.int32).reshape(1)
    own_rows = layer_inputs[0]
    swapped = lax.ppermute(own_rows, "tp", [(0, 1), (1, 0)])
    packed = call(
        functools.partial(pack_body, planes, slices, width),
        shape((planes, AUX + depth, owned), BF),
        out_weights[0].reshape(slices, planes, width, depth),
        short_weights[0],
        long_filters[0],
    )
    packed = lax.all_to_all(packed, "pipe", 0, 0, tiled=True)
    scattered = call(
        functools.partial(scatter_body, planes, slices, width),
        shape((planes, tokens, owned), BF),
        tp_index,
        own_rows,
        swapped,
        in_specs=[pl.BlockSpec(memory_space=pltpu.SMEM)]
        + [pl.BlockSpec(memory_space=pltpu.VMEM)] * 2,
    )

    def gathered(source, first, last):
        pieces = lax.all_gather(source[first : last + 1, AUX:], "seq", axis=0)
        return pieces.reshape(blocks, last + 1 - first, planes, width, owned)

    copies = jnp.broadcast_to(packed[top, AUX:][None], (blocks, depth, owned))
    pieces = lax.all_to_all(copies, "seq", 0, 0, tiled=True)
    first_weights = pieces.reshape(blocks, 1, planes, width, owned)
    first_weights, scattered = lax.optimization_barrier((first_weights, scattered))
    rows = lax.all_to_all(scattered, "pipe", 0, 0, tiled=True)
    before = from_before(rows, 1)
    before2 = from_before(rows[:, tokens - PAD :], 2)
    after = from_next(rows[:, :PAD], 1)

    def whole(x):
        return pl.BlockSpec(x.shape, lambda i: (0,) * len(x.shape))

    def plane(x, p, count, at=0):
        return pl.BlockSpec((None, count, x.shape[2]), lambda i, p=p, at=at: (p, at, 0))

    def own_block(p):
        return plane(rows, p, tokens)

    def aux_block(p):
        return plane(packed, p, AUX)

    def recomputed(p, earlier):
        results = (shape((4 * REACH, owned), F32), shape((groups * KL + WIN, owned), BF))
        return call(
            functools.partial(recompute_body, groups),
            results,
            rows,
            earlier,
            before2,
            after,
            packed,
            grid=(1,),
            in_specs=[
                own_block(p),
                plane(earlier, p, tokens),
                plane(before2, p, PAD),
                plane(after, p, PAD),
                aux_block(p),
            ],
            out_specs=tuple(whole(r) for r in results),
            scratch_shapes=[
                pltpu.VMEM((2 * KL + 2 * PAD, owned), F32),
                pltpu.VMEM((groups * KL, WIN), BF),
            ],
        )

    starts = call(
        functools.partial(shuffle_body, planes, width),
        shape((planes, tokens, owned), BF),
        out_grad,
    )
    grad = lax.dynamic_index_in_dim(starts, lax.axis_index("pipe"), 0, keepdims=False)
    swap = [(0, 1), (1, 0)]
    other = lax.ppermute(grad, "tp", swap)

    saved = {top: recomputed(top, before)}
    weights = {top: (first_weights, 0)}
    last = planes - 2
    for size in (1, 2, 2, planes):
        first = max(0, last - size + 1)
        if last >= first:
            group = gathered(packed, first, last)
            weights.update({p: (group, p - first) for p in range(first, last + 1)})
        last = first - 1

    def filter_sums(p, operands, sums):
        halves = owned // TILE
        result = shape((planes * halves, AUX, TILE), BF)
        specs = [whole(x) for x in operands]
        specs += [own_block(p), plane(before, p, PAD, tokens // PAD - 1)]
        operands = [*operands, rows, before]
        aliases = {}
        if sums is not None:
            aliases = {len(operands): 0}
            operands.append(sums)
            specs.append(pl.BlockSpec(memory_space=pl.ANY))
        return call(
            functools.partial(filters_body, groups),
            result,
            *operands,
            grid=(1,),
            in_specs=specs,
            out_specs=pl.BlockSpec((halves, AUX, TILE), lambda i, p=p: (p, 0, 0)),
            input_output_aliases=aliases,
            scratch_shapes=[
                pltpu.VMEM((KL + PAD, owned), F32),
                pltpu.VMEM((TILE // GW * KL, WIN), F32),
            ],
        )

    outs = [None] * planes
    sums = None
    late = None
    for p in range(planes - 1, -1, -1):
        group, at = weights[p]
        features, back = saved[p]
        if p + 1 < planes:
            other = lax.ppermute(grad, "tp", swap)
        partial = pl.pallas_call(
            project_body,
            out_shape=shape((planes, tokens, owned), BF),
            grid_spec=pltpu.PrefetchScalarGridSpec(
                num_scalar_prefetch=1,
                grid=(2,),
                in_specs=[
                    pl.BlockSpec((tokens, owned), lambda z, t: (0, 0)),
                    pl.BlockSpec((tokens, owned), lambda z, t: (0, 0)),
                    pl.BlockSpec(
                        (blocks, 1, planes // 2, width, owned), lambda z, t, at=at: (0, at, z, 0, 0)
                    ),
                ],
                out_specs=pl.BlockSpec((planes // 2, tokens, owned), lambda z, t: (z, 0, 0)),
            ),
            compiler_params=pltpu.CompilerParams(vmem_limit_bytes=VMEM_LIMIT),
            interpret=INTERPRET,
        )(tp_index, grad, other, group)
        if p == top:
            partial, rows = lax.optimization_barrier((partial, rows))
        parts = lax.all_to_all(partial, "pipe", 0, 0, tiled=True)
        send, dgate, early = call(
            gate_body,
            (
                shape((KL + PAD, owned), BF),
                shape((KL, owned), BF),
                shape((PAD, owned), BF),
            ),
            parts,
            features,
        )
        near = from_next(send, 1)
        far = from_next(early, 2)
        if late is not None:
            send, late[0] = lax.optimization_barrier((send, late[0]))
            sums = filter_sums(p + 1, late, sums)
            near, sums = lax.optimization_barrier((near, sums))
        if 0 < p < top - 1 and weights[p - 1][0] is not group:
            near, fetched = lax.optimization_barrier((near, weights[p - 1][0]))
            weights.update(
                {q: (fetched, i) for q, (g, i) in weights.items() if g is weights[p - 1][0]}
            )
        if p > 0:
            send, earlier = lax.optimization_barrier((send, before))
            saved[p - 1] = recomputed(p - 1, earlier)
            near, saved[p - 1] = lax.optimization_barrier((near, saved[p - 1]))
        results = (shape((KL, owned), BF), shape((3 * KL, owned), F32))
        operands = (send, dgate, near, far, features, back, packed, grad)
        new_grad, trail = call(
            functools.partial(finish_body, groups),
            results,
            *operands,
            grid=(1,),
            in_specs=[aux_block(p) if x is packed else whole(x) for x in operands],
            out_specs=tuple(whole(r) for r in results),
            scratch_shapes=[pltpu.VMEM((REACH, owned), F32)] * 3,
        )
        late = [trail, send, back]
        outs[p] = new_grad
        grad = new_grad

    sums = filter_sums(0, late, sums)
    exchanged = lax.all_to_all(sums, "seq", 0, 0, tiled=True)
    summed = call(
        functools.partial(sum_body, blocks), shape((blocks, AUX, TILE), BF), exchanged
    )
    summed = lax.all_to_all(summed, "seq", 0, 0, tiled=True)
    merged = call(merge_body, shape((planes, tokens + AUX, owned), BF), summed, *outs)
    results = lax.all_to_all(merged, "pipe", 0, 0, tiled=True)
    input_grad, short_result, long_result = call(
        functools.partial(spread_body, slices, width),
        (shape((tokens, half), BF), shape((KS, 8, half), F32), shape((dims, KL), F32)),
        results,
    )
    return input_grad[None], short_result[None, :, :3], long_result[None]


def solution(mesh):
    in_specs = (
        P("pipe", ("seq", "tp"), None),
        P("seq", "tp"),
        P("pipe", None, None, "tp"),
        P("pipe", "tp", None),
        P("pipe", "tp", "seq"),
    )
    out_specs = (P("pipe", "seq", "tp"), P("pipe", None, None, "tp"), P("pipe", "tp", None))
    return jax.shard_map(
        per_device, mesh=mesh, in_specs=in_specs, out_specs=out_specs, check_vma=False
    )
```

```python
import functools

import jax
import jax.numpy as jnp
from jax import lax
from jax.experimental import pallas as pl
from jax.experimental.pallas import tpu as pltpu
from jax.sharding import PartitionSpec as P

KL = 128
KS = 7
TILE = 128
GW = 16
AUX = 48
EDGE = 8
REACH = KL + EDGE
PAD = 16
WIN = 2 * KL
BF = jnp.bfloat16
F32 = jnp.float32
VMEM_LIMIT = 24 * 1024 * 1024
INTERPRET = False


def call(body, out_shape, *args, **kwargs):
    return pl.pallas_call(
        body,
        out_shape=out_shape,
        compiler_params=pltpu.CompilerParams(vmem_limit_bytes=VMEM_LIMIT),
        interpret=INTERPRET,
        **kwargs,
    )(*args)


def shape(dims, dtype):
    return jax.ShapeDtypeStruct(dims, dtype)


def dot(a, b):
    return jnp.dot(a, b, preferred_element_type=F32)


def dot_nt(a, b):
    return lax.dot_general(a, b, (((1,), (1,)), ((), ())), preferred_element_type=F32)


def swap_matrix(width):
    size = TILE // width
    n = size * TILE
    row = lax.broadcasted_iota(jnp.int32, (n, n), 0)
    col = lax.broadcasted_iota(jnp.int32, (n, n), 1)
    a, b, j = row // TILE, (row // width) % size, row % width
    return (col == b * TILE + a * width + j).astype(F32).astype(BF)


def split_owned(x, planes, width, matrix):
    step = planes * width
    slices = x.shape[1] // step
    size = TILE // width
    pieces = [[None] * (slices // size) for _ in range(planes)]
    for a in range(slices // size):
        for b in range(planes // size):
            tiles = [
                x[:, (a * size + i) * step + b * TILE : (a * size + i) * step + (b + 1) * TILE]
                for i in range(size)
            ]
            moved = dot(jnp.concatenate(tiles, axis=1), matrix).astype(BF)
            for i in range(size):
                pieces[b * size + i][a] = moved[:, i * TILE : (i + 1) * TILE]
    return [jnp.concatenate(p, axis=1) for p in pieces]


def join_owned(parts, width, matrix):
    planes = len(parts)
    size = TILE // width
    slices = parts[0].shape[1] // width
    out = [[None] * (planes // size) for _ in range(slices)]
    for a in range(slices // size):
        for b in range(planes // size):
            tiles = [parts[b * size + i][:, a * TILE : (a + 1) * TILE] for i in range(size)]
            moved = dot(jnp.concatenate(tiles, axis=1), matrix)
            for i in range(size):
                out[a * size + i][b] = moved[:, i * TILE : (i + 1) * TILE]
    return jnp.concatenate([jnp.concatenate(o, axis=1) for o in out], axis=1)


def filter_rows(slices, planes, per):
    n = slices * planes * per
    row = lax.broadcasted_iota(jnp.int32, (n, n), 0)
    col = lax.broadcasted_iota(jnp.int32, (n, n), 1)
    z, k, g = row // (slices * per), (row // per) % slices, row % per
    return (col == k * planes * per + z * per + g).astype(F32).astype(BF)


def pack_body(planes, slices, width, tp_ref, w_ref, sw_ref, lf_ref, x_ref, other_ref, out_ref):
    owned = slices * width
    depth = planes * width
    half = slices * depth
    count = x_ref.shape[0]
    matrix = swap_matrix(width)
    tp = tp_ref[0]
    start = pl.multiple_of(tp * half, TILE)
    for source, place in ((x_ref, tp), (other_ref, 1 - tp)):
        pieces = split_owned(source[:, pl.ds(start, half)], planes, width, matrix)
        at = pl.multiple_of(place * count, PAD)
        for z in range(planes):
            out_ref[z, pl.ds(at, count), :] = pieces[z]
    for z in range(planes):
        block = w_ref[:, z].reshape(owned, depth)
        turned = block.astype(F32).T.astype(BF)
        low = KL + z * width
        out_ref[:, low : low + width, :] = turned.reshape(planes, width, owned)
    base = KL + depth
    taps = [sw_ref[j].astype(F32) for j in range(KS)]
    taps.append(jnp.zeros((32 - 3 * KS, half), F32))
    taps = split_owned(jnp.concatenate(taps, axis=0).astype(BF), planes, width, matrix)
    per = width // GW
    filters = dot(filter_rows(slices, planes, per), lf_ref[...]).astype(BF)
    groups = slices * per
    for z in range(planes):
        out_ref[z, base : base + 32, :] = taps[z]
        out_ref[z, base + 32 : base + AUX, :] = jnp.zeros((GW, owned), BF)
        out_ref[z, base + 32 : base + 32 + groups, :KL] = filters[z * groups : (z + 1) * groups]


def shuffle_body(planes, width, x_ref, out_ref):
    pieces = split_owned(x_ref[...], planes, width, swap_matrix(width))
    for z in range(planes):
        out_ref[z] = pieces[z]


def grouped(toeplitz, rows_per, source, groups):
    channels = source.shape[1]
    tiles = []
    for u in range(channels // TILE):
        per = TILE // GW
        full = dot(toeplitz[u * per * rows_per : (u + 1) * per * rows_per], source[:, u * TILE : (u + 1) * TILE])
        lane = lax.broadcasted_iota(jnp.int32, (rows_per, TILE), 1) // GW
        merged = full[:rows_per]
        for g in range(1, per):
            merged = jnp.where(lane == g, full[g * rows_per : (g + 1) * rows_per], merged)
        tiles.append(merged)
    return jnp.concatenate(tiles, axis=1)


def edge_rows(ref, groups):
    return jnp.concatenate(
        [ref[g * KL + KL - PAD : (g + 1) * KL, :] for g in range(groups)], axis=0
    )


def recompute_body(
    groups, own_ref, prev_ref, prev2_ref, next_ref, aux_ref, features_ref, back_ref, rows_ref, band_ref,
):
    rows_ref[0:PAD, :] = prev2_ref[...].astype(F32)
    rows_ref[PAD : PAD + KL, :] = prev_ref[...].astype(F32)
    rows_ref[PAD + KL : PAD + 2 * KL, :] = own_ref[...].astype(F32)
    rows_ref[PAD + 2 * KL :, :] = next_ref[...].astype(F32)
    taps = aux_ref[0:32, :].astype(F32)

    def feature(f, first, count):
        start = PAD + KL + first
        total = taps[f : f + 1] * rows_ref[start : start + count, :]
        for j in range(1, KS):
            total = total + taps[3 * j + f : 3 * j + f + 1] * rows_ref[start - j : start - j + count, :]
        return total

    features_ref[0:REACH, :] = feature(0, 0, REACH)
    key_tail = feature(1, 0, REACH)
    value_tail = feature(2, 0, REACH)
    features_ref[REACH : 2 * REACH, :] = key_tail
    features_ref[2 * REACH : 3 * REACH, :] = value_tail
    kv = jnp.concatenate([feature(1, -KL, KL) * feature(2, -KL, KL), key_tail * value_tail], axis=0)
    window = kv[:WIN].astype(BF)
    late = kv[EDGE : EDGE + WIN].astype(BF)

    filters = aux_ref[32 : 32 + groups, :KL]
    tap = lax.broadcasted_iota(jnp.int32, (KL, WIN), 0)
    lane = lax.broadcasted_iota(jnp.int32, (KL, WIN), 1)
    ahead = dot(filters, (lane == KL - tap).astype(F32).astype(BF))
    behind = dot(filters, (lane == tap).astype(F32).astype(BF))
    for g in range(groups):
        wide = jnp.broadcast_to(ahead[g : g + 1], (KL, WIN))
        band_ref[g * KL : (g + 1) * KL, :] = pltpu.roll(wide, 0, 1, stride=1, stride_axis=0).astype(BF)
        wide = jnp.broadcast_to(behind[g : g + 1], (KL, WIN))
        back_ref[g * KL : (g + 1) * KL, :] = pltpu.roll(wide, 0, 1, stride=1, stride_axis=0).astype(BF)
    features_ref[3 * REACH : 3 * REACH + KL, :] = grouped(band_ref, KL, window, groups)
    features_ref[3 * REACH + KL :, :] = grouped(edge_rows(band_ref, groups), PAD, late, groups)[PAD - EDGE :]
    source = lax.broadcasted_iota(jnp.int32, (WIN, WIN), 0)
    target = lax.broadcasted_iota(jnp.int32, (WIN, WIN), 1)
    mirror = (source + target == WIN - 1).astype(F32).astype(BF)
    back_ref[groups * KL :, :] = dot(mirror, window).astype(BF)


def project_body(tp_ref, own_ref, other_ref, w_ref, out_ref):
    first = tp_ref[0] == 0
    own, other = own_ref[...], other_ref[...]
    rows = jnp.concatenate([jnp.where(first, own, other), jnp.where(first, other, own)], axis=1)
    slices, _, count, width, owned = w_ref.shape
    for z in range(count):
        out_ref[z] = dot(rows, w_ref[:, 0, z].reshape(slices * width, owned)).astype(BF)


def gate_body(parts_ref, features_ref, send_ref, dgate_ref, early_ref):
    total = parts_ref[0].astype(F32)
    for z in range(1, parts_ref.shape[0]):
        total = total + parts_ref[z].astype(F32)
    dgate = total.astype(BF)
    dmixed = (dgate.astype(F32) * features_ref[0:KL, :]).astype(BF)
    send_ref[0:KL, :] = dmixed
    send_ref[KL:, :] = dgate[:PAD]
    dgate_ref[...] = dgate
    early_ref[...] = dmixed[:PAD]


def finish_body(
    groups, send_ref, dgate_ref, near_ref, far_ref, features_ref, back_ref, aux_ref, grad_ref,
    out_ref, trail_ref, d0_ref, d1_ref, d2_ref,
):
    rows = jnp.concatenate(
        [send_ref[0:KL, :], near_ref[0:KL, :], far_ref[...]], axis=0
    )
    window = rows[:WIN]
    late = rows.astype(F32)[EDGE : EDGE + WIN].astype(BF)
    main = grouped(back_ref, KL, window, groups)
    tail = grouped(edge_rows(back_ref, groups), PAD, late, groups)[PAD - EDGE :]
    key, value, mixed = REACH, 2 * REACH, 3 * REACH
    d0_ref[0:KL, :] = dgate_ref[...].astype(F32) * features_ref[mixed : mixed + KL, :]
    d0_ref[KL:, :] = near_ref[KL:, :].astype(F32)[:EDGE] * features_ref[mixed + KL :, :]
    d1_ref[0:KL, :] = main * features_ref[value : value + KL, :]
    d1_ref[KL:, :] = tail * features_ref[value + KL : mixed, :]
    d2_ref[0:KL, :] = main * features_ref[key : key + KL, :]
    d2_ref[KL:, :] = tail * features_ref[key + KL : value, :]
    taps = aux_ref[0:32, :].astype(F32)
    total = grad_ref[...].astype(F32)
    for f, ref in enumerate((d0_ref, d1_ref, d2_ref)):
        trail_ref[f * KL : (f + 1) * KL, :] = ref[0:KL, :]
        for j in range(KS):
            total = total + taps[3 * j + f : 3 * j + f + 1] * ref[j : j + KL, :]
    out_ref[...] = total.astype(BF)


def filters_body(
    groups, trail_ref, send_ref, back_ref, own_ref, prev_ref, *refs,
):
    out_ref, rows_ref, skew_ref = refs[-3:]
    channels = own_ref.shape[1]
    rows_ref[0:PAD, :] = prev_ref[...].astype(F32)
    rows_ref[PAD:, :] = own_ref[...].astype(F32)
    sums = []
    for j in range(KS):
        source = rows_ref[PAD - j : PAD - j + KL, :]
        for f in range(3):
            grads = trail_ref[f * KL : (f + 1) * KL, :]
            sums.append(jnp.sum(grads * source, axis=0, keepdims=True))
    sums.append(jnp.zeros((32 - 3 * KS, channels), F32))
    short = jnp.concatenate(sums, axis=0).astype(BF)
    for u in range(channels // TILE):
        out_ref[u, 0:32, :] = short[:, u * TILE : (u + 1) * TILE]
    lags = []
    per = TILE // GW
    lane = lax.broadcasted_iota(jnp.int32, (KL, TILE), 1) // GW
    for u in range(channels // TILE):
        grad = send_ref[0:KL, u * TILE : (u + 1) * TILE].astype(F32)
        stacked = jnp.concatenate(
            [jnp.where(lane == g, grad, 0.0).astype(BF) for g in range(per)], axis=0
        )
        skew_ref[...] = dot_nt(stacked, back_ref[groups * KL :, u * TILE : (u + 1) * TILE])
        for g in range(per):
            rolled = pltpu.roll(skew_ref[g * KL : (g + 1) * KL, :], 0, 1, stride=1, stride_axis=0)
            lags.append(jnp.sum(rolled, axis=0, keepdims=True))
    if groups < GW:
        lags.append(jnp.zeros((GW - groups, WIN), F32))
    sums = pltpu.roll(jnp.concatenate(lags, axis=0), WIN - (KL - 1), 1)
    long = sums[:, :KL].astype(BF)
    for u in range(channels // TILE):
        out_ref[u, 32:AUX, :] = long


def sum_body(copies, in_ref, out_ref):
    total = in_ref[0].astype(F32)
    for s in range(1, in_ref.shape[0]):
        total = total + in_ref[s].astype(F32)
    value = total.astype(BF)
    for s in range(copies):
        out_ref[s] = value


def merge_body(sums_ref, *refs):
    grads, out_ref = refs[:-1], refs[-1]
    halves = sums_ref.shape[0] // len(grads)
    for p, ref in enumerate(grads):
        out_ref[p, :KL, :] = ref[...]
        for u in range(halves):
            out_ref[p, KL:, u * TILE : (u + 1) * TILE] = sums_ref[p * halves + u]


def spread_body(slices, width, in_ref, grad_ref, short_ref, long_ref):
    planes = in_ref.shape[0]
    matrix = swap_matrix(width)
    grad_ref[...] = join_owned([in_ref[z, :KL] for z in range(planes)], width, matrix).astype(BF)
    short = join_owned([in_ref[z, KL : KL + 32] for z in range(planes)], width, matrix)
    for j in range(KS):
        short_ref[j, 0:3, :] = short[3 * j : 3 * j + 3]
    per = width // GW
    groups = slices * per
    stacked = jnp.concatenate(
        [in_ref[z, KL + 32 : KL + 32 + groups, :KL] for z in range(planes)], axis=0
    )
    mover = filter_rows(slices, planes, per)
    long_ref[...] = lax.dot_general(
        mover, stacked, (((0,), (0,)), ((), ())), preferred_element_type=F32
    )


def from_next(x, by):
    size = lax.axis_size("seq")
    return lax.ppermute(x, "seq", [(i, i - by) for i in range(by, size)])


def from_before(x, by):
    size = lax.axis_size("seq")
    return lax.ppermute(x, "seq", [(i, i + by) for i in range(size - by)])


def per_device(layer_inputs, out_grad, short_weights, long_filters, out_weights):
    planes = lax.axis_size("pipe")
    blocks = lax.axis_size("seq")
    depth = out_weights.shape[2]
    half = out_grad.shape[1]
    width = depth // planes
    slices = half // depth
    owned = slices * width
    groups = owned // GW
    tokens = out_grad.shape[0]
    dims = long_filters.shape[1]

    tp_index = lax.axis_index("tp").astype(jnp.int32).reshape(1)
    own_rows = layer_inputs[0]
    swapped = lax.ppermute(own_rows, "tp", [(0, 1), (1, 0)])
    packed = pl.pallas_call(
        functools.partial(pack_body, planes, slices, width),
        out_shape=shape((planes, tokens + depth + AUX, owned), BF),
        in_specs=[pl.BlockSpec(memory_space=pltpu.SMEM)]
        + [pl.BlockSpec(memory_space=pltpu.VMEM)] * 5,
        compiler_params=pltpu.CompilerParams(vmem_limit_bytes=VMEM_LIMIT),
        interpret=INTERPRET,
    )(
        tp_index,
        out_weights[0].reshape(slices, planes, width, depth),
        short_weights[0],
        long_filters[0],
        own_rows,
        swapped,
    )
    packed = lax.all_to_all(packed, "pipe", 0, 0, tiled=True)
    top = planes - 1

    before2 = from_before(packed[:, tokens - PAD : tokens], 2)
    after = from_next(packed[:, :PAD], 1)

    def whole(x):
        return pl.BlockSpec(x.shape, lambda i: (0,) * len(x.shape))

    def plane(x, p, count, at=0):
        return pl.BlockSpec((None, count, x.shape[2]), lambda i, p=p, at=at: (p, at, 0))

    def own_block(p):
        return plane(packed, p, tokens)

    def aux_block(p):
        return plane(packed, p, AUX, (tokens + depth) // AUX)

    def recomputed(p, before, at):
        results = (shape((4 * REACH, owned), F32), shape((groups * KL + WIN, owned), BF))
        return call(
            functools.partial(recompute_body, groups),
            results,
            packed,
            before,
            before2,
            after,
            packed,
            grid=(1,),
            in_specs=[
                own_block(p),
                plane(before, at, tokens),
                plane(before2, p, PAD),
                plane(after, p, PAD),
                aux_block(p),
            ],
            out_specs=tuple(whole(r) for r in results),
            scratch_shapes=[
                pltpu.VMEM((2 * KL + 2 * PAD, owned), F32),
                pltpu.VMEM((groups * KL, WIN), BF),
            ],
        )

    def gathered(source, first, last):
        pieces = lax.all_gather(source[first : last + 1, tokens : tokens + depth], "seq", axis=0)
        return pieces.reshape(blocks, last + 1 - first, planes, width, owned)

    starts = call(
        functools.partial(shuffle_body, planes, width),
        shape((planes, tokens, owned), BF),
        out_grad,
    )
    grad = lax.dynamic_index_in_dim(starts, lax.axis_index("pipe"), 0, keepdims=False)
    swap = [(0, 1), (1, 0)]
    other = lax.ppermute(grad, "tp", swap)

    copies = jnp.broadcast_to(packed[top, tokens : tokens + depth][None], (blocks, depth, owned))
    copies, later = lax.optimization_barrier((copies, packed))
    pieces = lax.all_to_all(copies, "seq", 0, 0, tiled=True)
    first_weights = pieces.reshape(blocks, 1, planes, width, owned)
    nearest = from_before(packed[top:, :tokens], 1)
    first_weights, nearest, before2, after, source, grad, other = lax.optimization_barrier(
        (first_weights, nearest, before2, after, packed, grad, other)
    )
    before = {top: (nearest, 0)}
    others = from_before(source[:top, :tokens], 1)
    before.update({p: (others, p) for p in range(top)})
    saved = {top: recomputed(top, *before[top])}
    weights = {top: (first_weights, 0)}
    last = planes - 2
    for size in (1, 2, 2, planes):
        first = max(0, last - size + 1)
        if last >= first:
            group = gathered(later, first, last)
            weights.update({p: (group, p - first) for p in range(first, last + 1)})
        last = first - 1

    def filter_sums(p, operands, sums):
        halves = owned // TILE
        result = shape((planes * halves, AUX, TILE), BF)
        earlier, at = before[p]
        specs = [whole(x) for x in operands]
        specs += [own_block(p), plane(earlier, at, PAD, tokens // PAD - 1)]
        operands = [*operands, packed, earlier]
        aliases = {}
        if sums is not None:
            aliases = {len(operands): 0}
            operands.append(sums)
            specs.append(pl.BlockSpec(memory_space=pl.ANY))
        return call(
            functools.partial(filters_body, groups),
            result,
            *operands,
            grid=(1,),
            in_specs=specs,
            out_specs=pl.BlockSpec((halves, AUX, TILE), lambda i, p=p: (p, 0, 0)),
            input_output_aliases=aliases,
            scratch_shapes=[
                pltpu.VMEM((KL + PAD, owned), F32),
                pltpu.VMEM((TILE // GW * KL, WIN), F32),
            ],
        )

    outs = [None] * planes
    sums = None
    late = None
    for p in range(planes - 1, -1, -1):
        group, at = weights[p]
        features, back = saved[p]
        if p + 1 < planes:
            other = lax.ppermute(grad, "tp", swap)
        partial = pl.pallas_call(
            project_body,
            out_shape=shape((planes, tokens, owned), BF),
            grid_spec=pltpu.PrefetchScalarGridSpec(
                num_scalar_prefetch=1,
                grid=(2,),
                in_specs=[
                    pl.BlockSpec((tokens, owned), lambda z, t: (0, 0)),
                    pl.BlockSpec((tokens, owned), lambda z, t: (0, 0)),
                    pl.BlockSpec(
                        (blocks, 1, planes // 2, width, owned), lambda z, t, at=at: (0, at, z, 0, 0)
                    ),
                ],
                out_specs=pl.BlockSpec((planes // 2, tokens, owned), lambda z, t: (z, 0, 0)),
            ),
            compiler_params=pltpu.CompilerParams(vmem_limit_bytes=VMEM_LIMIT),
            interpret=INTERPRET,
        )(tp_index, grad, other, group)
        parts = lax.all_to_all(partial, "pipe", 0, 0, tiled=True)
        send, dgate, early = call(
            gate_body,
            (
                shape((KL + PAD, owned), BF),
                shape((KL, owned), BF),
                shape((PAD, owned), BF),
            ),
            parts,
            features,
        )
        near = from_next(send, 1)
        far = from_next(early, 2)
        if late is not None:
            send, late[0] = lax.optimization_barrier((send, late[0]))
            sums = filter_sums(p + 1, late, sums)
            near, sums = lax.optimization_barrier((near, sums))
        if p > 0:
            earlier, at = before[p - 1]
            send, earlier = lax.optimization_barrier((send, earlier))
            saved[p - 1] = recomputed(p - 1, earlier, at)
            near, saved[p - 1] = lax.optimization_barrier((near, saved[p - 1]))
        results = (shape((KL, owned), BF), shape((3 * KL, owned), F32))
        operands = (send, dgate, near, far, features, back, packed, grad)
        new_grad, trail = call(
            functools.partial(finish_body, groups),
            results,
            *operands,
            grid=(1,),
            in_specs=[aux_block(p) if x is packed else whole(x) for x in operands],
            out_specs=tuple(whole(r) for r in results),
            scratch_shapes=[pltpu.VMEM((REACH, owned), F32)] * 3,
        )
        late = [trail, send, back]
        outs[p] = new_grad
        grad = new_grad

    sums = filter_sums(0, late, sums)
    exchanged = lax.all_to_all(sums, "seq", 0, 0, tiled=True)
    summed = call(
        functools.partial(sum_body, blocks), shape((blocks, AUX, TILE), BF), exchanged
    )
    summed = lax.all_to_all(summed, "seq", 0, 0, tiled=True)
    merged = call(merge_body, shape((planes, tokens + AUX, owned), BF), summed, *outs)
    results = lax.all_to_all(merged, "pipe", 0, 0, tiled=True)
    input_grad, short_result, long_result = call(
        functools.partial(spread_body, slices, width),
        (shape((tokens, half), BF), shape((KS, 8, half), F32), shape((dims, KL), F32)),
        results,
    )
    return input_grad[None], short_result[None, :, :3], long_result[None]


def solution(mesh):
    in_specs = (
        P("pipe", ("seq", "tp"), None),
        P("seq", "tp"),
        P("pipe", None, None, "tp"),
        P("pipe", "tp", None),
        P("pipe", "tp", "seq"),
    )
    out_specs = (P("pipe", "seq", "tp"), P("pipe", None, None, "tp"), P("pipe", "tp", None))
    return jax.shard_map(
        per_device, mesh=mesh, in_specs=in_specs, out_specs=out_specs, check_vma=False
    )
```
